256 devices in a mesh: det: 64 (over x, z, core), row: 4 (over y).
Axes of the slice: x: 4, y: 4, z: 8, core: 2. Of those that a mesh axis runs over, the one named last changes fastest.
Arguments:
- images: bfloat16 [384, 3, 384, 384], P('det', None, 'row'), may hold values from -6 to 6
- warp_rows: bfloat16 [384, 3, 384, 384], P('det', None, 'row'), may hold values from -0.3125 to 0.3125
- warp_cols: bfloat16 [384, 3, 384, 384], P('det'), may hold values from -0.3125 to 0.3125
- psf_coef: float32 [384, 3, 21], P('det'), may hold values from -1.25 to 1.25
- taps: float32 [21, 21], replicated, may hold values from -1.25 to 1.25
- dest_patch: int32 [3456, 1], replicated, may hold values from 0 to 63; in each aligned block of 54 rows (0 to 53, 54 to 107, ...) at most 2 rows name the same one
- dest_block: int32 [3456], replicated, may hold values from 0 to 2
- weight_index: int32 [384, 3], replicated, may hold values from 0 to 7
- weight_table: float32 [8], replicated, may hold values from 0.25 to 4
- patch_home: int32 [64], replicated, may hold values from 0 to 63, each once
Outputs:
- difference: bfloat16 [384, 3, 384, 384], P('det', None, 'row')
- coadd: bfloat16 [64, 384, 384], P('det', 'row')
The draws below stay inside these ranges and needn't reach their ends.
Inputs may be any that keep to these rules, and one draw needn't show every extreme that they name: `dest_patch`: within the 54 rows of one device (an aligned block of rows), no patch is named more than 2 times. `patch_home`: each position once.
All inputs are finite; a program needn't handle non-finite values.
Results may differ from the reference program's by a relative error of at most 0.0082.
Values may be sent and summed in bfloat16 or wider, within the bound.
A program may use at most 128 MiB of HBM per device.

```python
import math
import jax
import jax.numpy as jnp
import numpy as np
from jax import lax

VISITS = 3
SIDE = 384
TILE = 128
KERNELS = 21
REACH = 10
LEVELS = 8
NDET = 384
TILES = 3
PIECES_DEV = 54
PIECES = 3456
PATCHES = 64
CAP = 2


def set_ends(array, own_key, low, top_value):
    index_at = [jax.random.randint(jax.random.fold_in(own_key, axis), (), 0, length) for axis, length in enumerate(array.shape)]
    main_axis = array.shape.index(max(array.shape))
    next_to = index_at[:main_axis] + [(index_at[main_axis] + 1) % array.shape[main_axis]] + index_at[main_axis + 1:]
    return array.at[tuple(index_at)].set(low).at[tuple(next_to)].set(top_value)


def block_levels(stream_key, extent, cuts, smallest, largest):
    gain = 1.0
    for axis_at, parts in cuts:
        heights = jax.random.uniform(jax.random.fold_in(jax.random.fold_in(stream_key, 6), axis_at), (parts,), jnp.float32, smallest / len(cuts), largest / len(cuts))
        gain = gain * jnp.repeat(jnp.exp(heights), extent[axis_at] // parts).reshape((-1,) + (1,) * (len(extent) - 1 - axis_at))
    return gain


def routed_block(rng, own, number, rows, count, top, most, skew):
    order = jax.random.permutation(rng, count)
    crowded, common = portions_of(count, rows * top, most, skew, True), portions_of(count, rows * top, most, skew, False)
    places = jnp.arange(count)

    def named(lengths, rotation):
        used = int((lengths > 0).sum())
        fixed = max(1, used // 4)
        passed = fixed + (places - fixed + rotation * (used - fixed)) % max(1, count - fixed)
        return jnp.zeros((count,), jnp.int32).at[order[jnp.where(places < fixed, places, passed)]].set(jnp.asarray(lengths, jnp.int32))

    lengths = jnp.where(number % 4 == 0, named(crowded, number // 4), named(common, number - number // 4 - 1))
    mixed = jax.random.permutation(jax.random.fold_in(own, 3), count)
    giver, sink = mixed[0:count // 2 * 2:2], mixed[1:count // 2 * 2:2]
    margin = jnp.minimum(lengths[giver] - 1, most - lengths[sink]) // 2
    margin = jnp.where((giver == order[0]) | (sink == order[0]) | (lengths[sink] == 0), 0, jnp.maximum(margin, 0))
    passed = jax.random.randint(jax.random.fold_in(own, 4), (count // 2,), 0, 1 << 20) % (margin + 1)
    lengths = lengths.at[giver].add(-passed).at[sink].add(passed)
    items = jnp.searchsorted(jnp.cumsum(lengths), jnp.arange(rows * top), side="right").astype(jnp.int32)
    grid = items.reshape(top, rows).T
    grid = grid[jax.random.permutation(jax.random.fold_in(own, 1), rows)]
    rotation = jax.random.randint(jax.random.fold_in(own, 2), (rows, 1), 0, top)
    return jnp.take_along_axis(grid, (jnp.arange(top)[None, :] + rotation) % top, axis=1)


def portions_of(amount, total, limit, lean, full):
    portions = [(1 << 20) // math.isqrt(rank ** lean) + 1 for rank in range(1, amount + 1)]
    largest = limit if full else min(limit, max(-(-total // amount), total * portions[0] // sum(portions)))
    least = 1 if total - largest >= amount - 1 else 0
    holding, rest = [largest] + [least] * (amount - 1), total - largest - least * (amount - 1)
    while rest > 0:
        candidates = [i for i in range(1, amount) if holding[i] < largest] or [i for i in range(1, amount) if holding[i] < limit]
        mass, remaining = sum([portions[i] for i in candidates]), rest
        for i in candidates:
            more = min(limit - holding[i], max(1, remaining * portions[i] // mass), rest)
            holding[i] = holding[i] + more
            rest = rest - more
    return np.array(holding)


def gaussian(own_key, shape, deviation, most, cuts=(), dtype=jnp.bfloat16):
    result = jax.random.normal(own_key, shape, jnp.float32) * deviation
    if len(cuts) > 0:
        result = block_levels(own_key, shape, cuts, -0.22, 0.18) * result
    return jnp.clip(result, min=-most, max=most).astype(dtype)


def setup_inputs(seed: int = 0) -> dict:
    keys = jax.random.split(jax.random.key(seed), 11)
    images = gaussian(keys[0], (NDET, VISITS, SIDE, SIDE), 1.0, 6.0, ((0, 64), (2, 4)))
    warp_rows = gaussian(keys[1], (NDET, VISITS, SIDE, SIDE), SIDE ** -0.5, 0.3125, ((0, 64), (2, 4)))
    warp_cols = gaussian(keys[2], (NDET, VISITS, SIDE, SIDE), SIDE ** -0.5, 0.3125, ((0, 64),))
    psf_coef = gaussian(keys[3], (NDET, VISITS, KERNELS), KERNELS ** -0.5, 1.25, ((0, 64),), jnp.float32)
    taps = gaussian(keys[4], (KERNELS, 2 * REACH + 1), (2 * REACH + 1) ** -0.5, 1.25, (), jnp.float32)
    dest_patch_keys = jax.random.split(jax.random.fold_in(keys[5], 1), PIECES // PIECES_DEV)
    dest_patch_turns = jax.random.permutation(jax.random.fold_in(keys[5], 3), PIECES // PIECES_DEV)
    dest_patch = jax.vmap(lambda own, number: routed_block(jax.random.fold_in(keys[5], 2), own, number, PIECES_DEV, PATCHES, 1, CAP, 2))(dest_patch_keys, dest_patch_turns).reshape((PIECES, 1))
    dest_block = set_ends(jax.random.randint(keys[6], (PIECES,), 0, TILES), jax.random.fold_in(keys[6], 1), 0, TILES - 1).astype(jnp.int32)
    weight_index = set_ends(jax.random.randint(keys[7], (NDET, VISITS), 0, LEVELS), jax.random.fold_in(keys[7], 1), 0, LEVELS - 1).astype(jnp.int32)
    weight_table = jnp.clip(jnp.exp(jax.random.uniform(keys[8], (LEVELS,), jnp.float32, math.log(0.25), math.log(4.0))), 0.25, 4.0)
    patch_home = jax.random.permutation(keys[9], PATCHES).astype(jnp.int32)
    return {"images": images, "warp_rows": warp_rows, "warp_cols": warp_cols, "psf_coef": psf_coef, "taps": taps, "dest_patch": dest_patch, "dest_block": dest_block, "weight_index": weight_index, "weight_table": weight_table, "patch_home": patch_home}


def rounded(value):
    return lax.optimization_barrier(value.astype(jnp.bfloat16)).astype(jnp.float32)


def correlate(signal, kernel):
    reach = (kernel.shape[2] - 1) // 2
    return lax.conv_general_dilated(signal, kernel, (1,), [(reach, reach)], precision=lax.Precision.HIGHEST)


def reference(images, warp_rows, warp_cols, psf_coef, taps, dest_patch, dest_block, weight_index, weight_table, patch_home):
    taps_half = rounded(taps)

    def match_image(inputs):
        image, rows_map, cols_map, coef_row = inputs
        col_warped = jnp.dot(image, cols_map, preferred_element_type=jnp.float32).astype(jnp.bfloat16)
        warped = rounded(jnp.dot(rows_map, col_warped, preferred_element_type=jnp.float32))
        conv_cols = rounded(correlate(warped[:, None, :], taps_half[:, None, :]))
        scaled = rounded(coef_row[:, None] * taps)
        conv_rows = correlate(jnp.transpose(conv_cols, (2, 1, 0)), scaled[None])
        return jnp.transpose(conv_rows[:, 0, :])

    image_count = NDET * VISITS
    matched = lax.map(match_image, (images.reshape(image_count, SIDE, SIDE), warp_rows.reshape(image_count, SIDE, SIDE), warp_cols.reshape(image_count, SIDE, SIDE), psf_coef.reshape(image_count, KERNELS)))
    weights = weight_table[weight_index].reshape(image_count)
    weighted = rounded(weights[:, None, None] * matched)
    pieces = weighted.reshape(image_count, SIDE, TILES, TILE).transpose(0, 2, 1, 3).reshape(PIECES, SIDE, TILE)
    segment_ids = (patch_home[dest_patch[:, 0]] * TILES + dest_block).astype(jnp.int32)
    numerator = jax.ops.segment_sum(pieces, segment_ids, num_segments=PATCHES * TILES)
    denominator = jax.ops.segment_sum(jnp.repeat(weights, TILES), segment_ids, num_segments=PATCHES * TILES)
    template = rounded(numerator / jnp.maximum(denominator, 1.0)[:, None, None])
    coadd = template.reshape(PATCHES, TILES, SIDE, TILE).transpose(0, 2, 1, 3).reshape(PATCHES, SIDE, SIDE).astype(jnp.bfloat16)
    local_template = template[segment_ids].reshape(image_count, TILES, SIDE, TILE).transpose(0, 2, 1, 3).reshape(image_count, SIDE, SIDE)
    difference = (matched - local_template).astype(jnp.bfloat16).reshape(NDET, VISITS, SIDE, SIDE)
    return difference, coadd
```

```python
import functools

import jax
import jax.numpy as jnp
from jax import lax
from jax.experimental import pallas as pl
from jax.experimental.pallas import tpu as pltpu
from jax.sharding import PartitionSpec as P

TILE = 128
HALF = 64
HALO = 16
GROUP = 4


def build_table(base_ref, image, keep, table_ref, offsets):
    for t in range(offsets - 2):
        row = jnp.broadcast_to(base_ref[image, pl.ds(t, 1), :], keep.shape)
        band = pltpu.roll(row, 0, 1, stride=1, stride_axis=0)
        band = jnp.where(keep, band, 0.0).astype(jnp.bfloat16)
        table_ref[pl.ds(t * TILE, keep.shape[0]), pl.ds(0, TILE)] = band
        table_ref[pl.ds((t + 2) * TILE, keep.shape[0]), pl.ds(TILE, TILE)] = band


def table_mask(span):
    rows = lax.broadcasted_iota(jnp.int32, (96, TILE), 0)
    lanes = lax.broadcasted_iota(jnp.int32, (96, TILE), 1)
    gap = rows - jnp.where(lanes >= HALF, lanes - HALF, lanes)
    return (gap >= 0) & (gap < span)


def convolve(warped, reach, window_ref, left_ref, table_ref, out_ref, image, offsets):
    rows, cols = warped.shape
    wide = jnp.concatenate([warped, jnp.zeros((rows, TILE), jnp.float32)], axis=1)
    even = pltpu.roll(wide, reach, 1)
    odd = pltpu.roll(wide, cols + TILE + reach - HALF, 1)
    tiles = cols // TILE
    groups = out_ref.shape[2] // GROUP
    for tile in range(tiles):
        window_ref[2 * tile] = even[:, tile * TILE : (tile + 1) * TILE]
        window_ref[2 * tile + 1] = odd[:, tile * TILE : (tile + 1) * TILE]
    for offset in range(offsets):
        start = HALO - reach + offset
        parts = [window_ref[w, pl.ds(start, groups, stride=GROUP), :] for w in range(2 * tiles)]
        left_ref[:, pl.ds(offset * TILE, TILE)] = jnp.concatenate(parts, axis=0).astype(jnp.bfloat16)
    product = jnp.dot(left_ref[...], table_ref[...], preferred_element_type=jnp.float32)
    low = lax.broadcasted_iota(jnp.int32, (groups, TILE), 1) < HALF
    for tile in range(tiles):
        for pair in range(2):
            first = product[(2 * tile) * groups : (2 * tile + 1) * groups, pair * TILE : (pair + 1) * TILE]
            second = product[(2 * tile + 1) * groups : (2 * tile + 2) * groups, pair * TILE : (pair + 1) * TILE]
            upper = jnp.where(low, first, pltpu.roll(second, HALF, 1))
            lower = jnp.where(low, pltpu.roll(first, HALF, 1), second)
            out_ref[image, tile, pl.ds(2 * pair, groups, stride=GROUP), :] = upper
            out_ref[image, tile, pl.ds(2 * pair + 1, groups, stride=GROUP), :] = lower


def match_kernel(reach, offsets, base_ref, rows_ref, full_ref, out_ref, window_ref, left_ref, table_ref):
    @pl.when(pl.program_id(0) == 0)
    def _():
        table_ref[...] = jnp.zeros_like(table_ref)

    build_table(base_ref, 0, table_mask(2 * reach + 1), table_ref, offsets)
    warped = jnp.dot(rows_ref[0], full_ref[0], preferred_element_type=jnp.float32)
    convolve(warped, reach, window_ref, left_ref, table_ref, out_ref, 0, offsets)


def match(base, rows_ext, full, reach):
    images, ext, cols = rows_ext.shape
    band = ext - 2 * HALO
    offsets = 2 * reach + GROUP
    return pl.pallas_call(
        functools.partial(match_kernel, reach, offsets),
        grid=(images,),
        in_specs=[
            pl.BlockSpec((1,) + base.shape[1:], lambda i: (i, 0, 0)),
            pl.BlockSpec((1, ext, cols), lambda i: (i, 0, 0)),
            pl.BlockSpec((1, cols, cols), lambda i: (i, 0, 0)),
        ],
        out_specs=pl.BlockSpec((1, cols // TILE, band, TILE), lambda i: (i, 0, 0, 0)),
        out_shape=jax.ShapeDtypeStruct((images, cols // TILE, band, TILE), jnp.float32),
        scratch_shapes=[
            pltpu.VMEM((2 * (cols // TILE), ext, TILE), jnp.float32),
            pltpu.VMEM((2 * (cols // TILE) * (band // GROUP), offsets * TILE), jnp.bfloat16),
            pltpu.VMEM((offsets * TILE, 2 * TILE), jnp.bfloat16),
        ],
        compiler_params=pltpu.CompilerParams(vmem_limit_bytes=48 << 20),
        name="match",
    )(base, rows_ext, full)


def collect_kernel(tiles, target_ref, weight_ref, matched_ref, dense_ref):
    image = pl.program_id(0)

    @pl.when(image == 0)
    def _():
        dense_ref[...] = jnp.zeros_like(dense_ref)

    for tile in range(tiles):
        piece = weight_ref[image] * matched_ref[0, tile]
        piece = piece.astype(jnp.bfloat16).astype(jnp.float32)
        target = target_ref[image * tiles + tile]
        dense_ref[target] = (dense_ref[target].astype(jnp.float32) + piece).astype(jnp.bfloat16)


def collect(targets, weights, matched, boxes):
    images, tiles, band, _ = matched.shape
    return pl.pallas_call(
        functools.partial(collect_kernel, tiles),
        grid_spec=pltpu.PrefetchScalarGridSpec(
            num_scalar_prefetch=2,
            grid=(images,),
            in_specs=[pl.BlockSpec((1, tiles, band, TILE), lambda i, *_: (i, 0, 0, 0))],
            out_specs=pl.BlockSpec((boxes, band, TILE), lambda i, *_: (0, 0, 0), pipeline_mode=pl.Buffered(1)),
        ),
        out_shape=jax.ShapeDtypeStruct((boxes, band, TILE), jnp.bfloat16),
        compiler_params=pltpu.CompilerParams(vmem_limit_bytes=32 << 20),
        name="collect",
    )(targets, weights, matched)


def subtract_kernel(tiles, target_ref, matched_ref, template_ref, out_ref):
    image = pl.program_id(0)
    for tile in range(tiles):
        target = target_ref[image * tiles + tile]
        lanes = pl.ds(tile * TILE, TILE)
        out_ref[0, :, lanes] = (matched_ref[0, tile] - template_ref[target].astype(jnp.float32)).astype(jnp.bfloat16)


def subtract(targets, matched, templates):
    images, tiles, band, _ = matched.shape
    return pl.pallas_call(
        functools.partial(subtract_kernel, tiles),
        grid_spec=pltpu.PrefetchScalarGridSpec(
            num_scalar_prefetch=1,
            grid=(images,),
            in_specs=[
                pl.BlockSpec((1, tiles, band, TILE), lambda i, *_: (i, 0, 0, 0)),
                pl.BlockSpec(templates.shape, lambda i, *_: (0, 0, 0), pipeline_mode=pl.Buffered(1)),
            ],
            out_specs=pl.BlockSpec((1, band, tiles * TILE), lambda i, *_: (i, 0, 0)),
        ),
        out_shape=jax.ShapeDtypeStruct((images, band, tiles * TILE), jnp.bfloat16),
        compiler_params=pltpu.CompilerParams(vmem_limit_bytes=32 << 20),
        name="subtract",
    )(targets, matched, templates)


def base_rows(psf_coef, taps):
    images = psf_coef.shape[0]
    kernels, span = taps.shape
    scaled = (psf_coef[:, :, None] * taps[None]).astype(jnp.bfloat16)
    by_tap = jnp.transpose(scaled, (0, 2, 1))
    lead = jnp.pad(by_tap, ((0, 0), (0, 1), (0, 0)))
    late = jnp.pad(by_tap, ((0, 0), (1, 0), (0, 0)))
    both = jnp.concatenate([lead, late], axis=2)
    lanes = jnp.arange(TILE)[None, :]
    taken = jnp.arange(span)[:, None]
    here = ((-taken) % TILE == lanes).astype(jnp.float32)
    there = (HALF - taken == lanes).astype(jnp.float32)
    half = taps.astype(jnp.bfloat16).astype(jnp.float32)
    placed = jnp.concatenate(
        [
            jnp.dot(half, here, precision=lax.Precision.HIGHEST),
            jnp.dot(half, there, precision=lax.Precision.HIGHEST),
        ],
        axis=0,
    ).astype(jnp.bfloat16)
    return jnp.einsum("itk,kc->itc", both, placed, preferred_element_type=jnp.float32)


def per_device(
    images,
    warp_rows,
    warp_cols,
    psf_coef,
    taps,
    dest_patch,
    dest_block,
    weight_index,
    weight_table,
    patch_home,
):
    dets, visits, band, cols = images.shape
    reach = (taps.shape[1] - 1) // 2
    tiles = cols // TILE
    count = dets * visits
    patches = patch_home.shape[0]
    me = lax.axis_index("det")
    row_size = lax.axis_size("row")

    rows = warp_rows.reshape(count, band, cols)
    up = [(i, i + 1) for i in range(row_size - 1)]
    down = [(j, i) for i, j in up]
    before = lax.ppermute(rows[:, band - HALO :], "row", up)
    after = lax.ppermute(rows[:, :HALO], "row", down)
    rows_ext = jnp.concatenate([before, rows, after], axis=1)
    col_warped = jnp.einsum(
        "nbs,nst->nbt",
        images.reshape(count, band, cols),
        warp_cols.reshape(count, cols, cols),
        preferred_element_type=jnp.float32,
    ).astype(jnp.bfloat16)
    full = lax.all_gather(col_warped, "row", axis=1, tiled=True)

    base = base_rows(psf_coef.reshape(count, -1), taps)
    matched = match(base, rows_ext, full, reach)

    levels = weight_table.shape[0]
    flat_index = weight_index.reshape(-1)
    weight_all = jnp.sum(
        jnp.where(flat_index[:, None] == jnp.arange(levels)[None, :], weight_table[None, :], 0.0), axis=1
    )
    weight_mine = lax.dynamic_slice_in_dim(weight_all, me * count, count, 0)
    patch_mine = lax.dynamic_slice_in_dim(dest_patch[:, 0], me * count * tiles, count * tiles, 0)
    block_mine = lax.dynamic_slice_in_dim(dest_block, me * count * tiles, count * tiles, 0)
    home_mine = jnp.sum(
        jnp.where(patch_mine[:, None] == jnp.arange(patches)[None, :], patch_home[None, :], 0), axis=1
    )
    targets = home_mine * tiles + block_mine
    my_patch = jnp.sum(jnp.where(patch_home == me, jnp.arange(patches), 0))
    to_mine = jnp.where(dest_patch[:, 0] == my_patch, dest_block, -1).reshape(-1, tiles)
    denominator = jnp.stack(
        [jnp.sum(jnp.where(to_mine == b, weight_all[:, None], 0.0)) for b in range(tiles)]
    )

    dense = collect(targets, weight_mine, matched, patches * tiles)
    numerator = lax.psum_scatter(dense, "det", scatter_dimension=0, tiled=True)
    template = (numerator.astype(jnp.float32) / jnp.maximum(denominator, 1.0)[:, None, None]).astype(jnp.bfloat16)
    coadd = jnp.transpose(template, (1, 0, 2)).reshape(1, band, cols)
    templates = lax.all_gather(template, "det", axis=0, tiled=True)
    difference = subtract(targets, matched, templates)
    return (difference.reshape(dets, visits, band, cols), coadd)


def solution(mesh):
    placed = (
        P("det", None, "row", None),
        P("det", None, "row", None),
        P("det", None, None, None),
        P("det", None, None),
        P(),
        P(),
        P(),
        P(),
        P(),
        P(),
    )
    return jax.shard_map(
        per_device,
        mesh=mesh,
        in_specs=placed,
        out_specs=(P("det", None, "row", None), P("det", "row", None)),
        check_vma=False,
    )
```

```python
import functools

import jax
import jax.numpy as jnp
from jax import lax
from jax.experimental import pallas as pl
from jax.experimental.pallas import tpu as pltpu
from jax.sharding import PartitionSpec as P

TILE = 128
HALF = 64
HALO = 16
GROUP = 4
DEPTH = 8
SPLIT = 128


def build_table(base_ref, image, keep, table_ref, offsets):
    for t in range(offsets - 2):
        row = jnp.broadcast_to(base_ref[image, pl.ds(t, 1), :], keep.shape)
        band = pltpu.roll(row, 0, 1, stride=1, stride_axis=0)
        band = jnp.where(keep, band, 0.0).astype(jnp.bfloat16)
        table_ref[pl.ds(t * TILE, keep.shape[0]), pl.ds(0, TILE)] = band
        table_ref[pl.ds((t + 2) * TILE, keep.shape[0]), pl.ds(TILE, TILE)] = band


def table_mask(span):
    rows = lax.broadcasted_iota(jnp.int32, (96, TILE), 0)
    lanes = lax.broadcasted_iota(jnp.int32, (96, TILE), 1)
    gap = rows - jnp.where(lanes >= HALF, lanes - HALF, lanes)
    return (gap >= 0) & (gap < span)


def convolve(warped, reach, window_ref, left_ref, table_ref, out_ref, image, offsets):
    rows, cols = warped.shape
    wide = jnp.concatenate([warped, jnp.zeros((rows, TILE), jnp.float32)], axis=1)
    even = pltpu.roll(wide, reach, 1)
    odd = pltpu.roll(wide, cols + TILE + reach - HALF, 1)
    tiles = cols // TILE
    groups = out_ref.shape[2] // GROUP
    for tile in range(tiles):
        window_ref[2 * tile] = even[:, tile * TILE : (tile + 1) * TILE]
        window_ref[2 * tile + 1] = odd[:, tile * TILE : (tile + 1) * TILE]
    for offset in range(offsets):
        start = HALO - reach + offset
        parts = [window_ref[w, pl.ds(start, groups, stride=GROUP), :] for w in range(2 * tiles)]
        left_ref[:, pl.ds(offset * TILE, TILE)] = jnp.concatenate(parts, axis=0).astype(jnp.bfloat16)
    product = jnp.dot(left_ref[...], table_ref[...], preferred_element_type=jnp.float32)
    low = lax.broadcasted_iota(jnp.int32, (groups, TILE), 1) < HALF
    for tile in range(tiles):
        for pair in range(2):
            first = product[(2 * tile) * groups : (2 * tile + 1) * groups, pair * TILE : (pair + 1) * TILE]
            second = product[(2 * tile + 1) * groups : (2 * tile + 2) * groups, pair * TILE : (pair + 1) * TILE]
            upper = jnp.where(low, first, pltpu.roll(second, HALF, 1))
            lower = jnp.where(low, pltpu.roll(first, HALF, 1), second)
            out_ref[image, tile, pl.ds(2 * pair, groups, stride=GROUP), :] = upper
            out_ref[image, tile, pl.ds(2 * pair + 1, groups, stride=GROUP), :] = lower


def match_kernel(reach, offsets, base_ref, rows_ref, full_ref, out_ref, window_ref, left_ref, table_ref):
    @pl.when(pl.program_id(0) == 0)
    def _():
        table_ref[...] = jnp.zeros_like(table_ref)

    build_table(base_ref, 0, table_mask(2 * reach + 1), table_ref, offsets)
    warped = jnp.dot(rows_ref[0], full_ref[0], preferred_element_type=jnp.float32)
    convolve(warped, reach, window_ref, left_ref, table_ref, out_ref, 0, offsets)


def match(base, rows_ext, full, reach):
    images, ext, cols = rows_ext.shape
    band = ext - 2 * HALO
    offsets = 2 * reach + GROUP
    return pl.pallas_call(
        functools.partial(match_kernel, reach, offsets),
        grid=(images,),
        in_specs=[
            pl.BlockSpec((1,) + base.shape[1:], lambda i: (i, 0, 0)),
            pl.BlockSpec((1, ext, cols), lambda i: (i, 0, 0)),
            pl.BlockSpec((1, cols, cols), lambda i: (i, 0, 0)),
        ],
        out_specs=pl.BlockSpec((1, cols // TILE, band, TILE), lambda i: (i, 0, 0, 0)),
        out_shape=jax.ShapeDtypeStruct((images, cols // TILE, band, TILE), jnp.float32),
        scratch_shapes=[
            pltpu.VMEM((2 * (cols // TILE), ext, TILE), jnp.float32),
            pltpu.VMEM((2 * (cols // TILE) * (band // GROUP), offsets * TILE), jnp.bfloat16),
            pltpu.VMEM((offsets * TILE, 2 * TILE), jnp.bfloat16),
        ],
        compiler_params=pltpu.CompilerParams(vmem_limit_bytes=48 << 20),
        name="match",
    )(base, rows_ext, full)


def collect_kernel(tiles, target_ref, weight_ref, matched_ref, dense_ref):
    image = pl.program_id(0)

    @pl.when(image == 0)
    def _():
        dense_ref[...] = jnp.zeros_like(dense_ref)

    for tile in range(tiles):
        piece = weight_ref[image] * matched_ref[0, tile]
        piece = piece.astype(jnp.bfloat16).astype(jnp.float32)
        target = target_ref[image * tiles + tile]
        dense_ref[target] = (dense_ref[target].astype(jnp.float32) + piece).astype(jnp.bfloat16)


def collect(targets, weights, matched, boxes):
    images, tiles, band, _ = matched.shape
    return pl.pallas_call(
        functools.partial(collect_kernel, tiles),
        grid_spec=pltpu.PrefetchScalarGridSpec(
            num_scalar_prefetch=2,
            grid=(images,),
            in_specs=[pl.BlockSpec((1, tiles, band, TILE), lambda i, *_: (i, 0, 0, 0))],
            out_specs=pl.BlockSpec((boxes, band, TILE), lambda i, *_: (0, 0, 0), pipeline_mode=pl.Buffered(1)),
        ),
        out_shape=jax.ShapeDtypeStruct((boxes, band, TILE), jnp.bfloat16),
        compiler_params=pltpu.CompilerParams(vmem_limit_bytes=32 << 20),
        name="collect",
    )(targets, weights, matched)


def subtract_kernel(tiles, target_ref, matched_ref, template_ref, out_ref):
    image = pl.program_id(0)
    for tile in range(tiles):
        target = target_ref[image * tiles + tile]
        lanes = pl.ds(tile * TILE, TILE)
        out_ref[0, :, lanes] = (matched_ref[0, tile] - template_ref[target].astype(jnp.float32)).astype(jnp.bfloat16)


def subtract(targets, matched, templates):
    images, tiles, band, _ = matched.shape
    return pl.pallas_call(
        functools.partial(subtract_kernel, tiles),
        grid_spec=pltpu.PrefetchScalarGridSpec(
            num_scalar_prefetch=1,
            grid=(images,),
            in_specs=[
                pl.BlockSpec((1, tiles, band, TILE), lambda i, *_: (i, 0, 0, 0)),
                pl.BlockSpec(templates.shape, lambda i, *_: (0, 0, 0), pipeline_mode=pl.Buffered(1)),
            ],
            out_specs=pl.BlockSpec((1, band, tiles * TILE), lambda i, *_: (i, 0, 0)),
        ),
        out_shape=jax.ShapeDtypeStruct((images, band, tiles * TILE), jnp.bfloat16),
        compiler_params=pltpu.CompilerParams(vmem_limit_bytes=32 << 20),
        name="subtract",
    )(targets, matched, templates)


def det_index(x, z, core, depth):
    return (x * depth + z) * 2 + core


class Links:
    def __init__(self, send_ref, recv_ref):
        self.send_ref, self.recv_ref = send_ref, recv_ref
        self.copies = {}

    def start(self, key, source, target, device):
        index = len(self.copies)
        copy = pltpu.make_async_remote_copy(
            src_ref=source,
            dst_ref=target,
            send_sem=self.send_ref.at[index],
            recv_sem=self.recv_ref.at[index],
            device_id=device,
            device_id_type=pl.DeviceIdType.MESH,
        )
        copy.start()
        self.copies[key] = copy

    def arrive(self, key):
        self.copies[key].wait_recv()

    def finish(self):
        for copy in self.copies.values():
            copy.wait_send()


def signed(place, step, way, size):
    return lax.rem(place + size + (step if way == 0 else -step), size)


def ring_reduce(links, tag, size, place, lead, rows, at, held_ref, whole_ref, half_ref, neighbour, base, finish):
    middle, half = size // 2, rows // 2

    def add(dest, extras, store):
        if base is not None:
            base(dest)

        def body(l, carry):
            for lo in (0, half):
                index = at(dest, l, lo, half)
                total = held_ref[index].astype(jnp.float32)
                if base is not None:
                    total = total + base.ref[base.index(dest, l, lo, half)].astype(jnp.float32)
                for ref, way, from_half in extras:
                    if not from_half:
                        total = total + ref[way, l, pl.ds(lo, half), :].astype(jnp.float32)
                    elif lo == way * half:
                        total = total + ref[way, l].astype(jnp.float32)
                store(l, lo, index, total)
            return carry

        lax.fori_loop(0, lead, body, 0)

    def put(l, lo, index, total):
        held_ref[index] = total.astype(jnp.bfloat16)

    far = signed(place, middle, 0, size)
    if base is not None:
        add(far, [], put)
    for way in (0, 1):
        links.start((tag, way, middle), held_ref.at[at(far, None, way * half, half)], half_ref.at[way], neighbour(way))
    yield
    for step in range(middle - 1, 0, -1):
        for way in (0, 1):
            dest = signed(place, step, way, size)
            links.arrive((tag, way, step + 1))
            source = (half_ref, way, True) if step + 1 == middle else (whole_ref.at[step], way, False)
            add(dest, [source], put)
            links.start(
                (tag, way, step), held_ref.at[at(dest, None, 0, rows)], whole_ref.at[step - 1, way], neighbour(way)
            )
        yield
    for way in (0, 1):
        links.arrive((tag, way, 1))
    add(place, [(whole_ref.at[0], 0, False), (whole_ref.at[0], 1, False)], put if finish is None else finish)
    yield


def ring_gather(links, tag, size, place, rows, view, neighbour, arrived):
    middle, half = size // 2, rows // 2
    for way in (0, 1):
        links.start((tag, way, 1), view(place, 0, rows), view(place, 0, rows), neighbour(way))
    arrived(place, 0)
    yield
    for step in range(1, middle):
        for way in (0, 1):
            origin = signed(place, step, 1 - way, size)
            links.arrive((tag, way, step))
            lo, length = (0, rows) if step + 1 < middle else (way * half, half)
            links.start((tag, way, step + 1), view(origin, lo, length), view(origin, lo, length), neighbour(way))
            arrived(origin, (step, way))
        yield
    for way in (0, 1):
        links.arrive((tag, way, middle))
    arrived(signed(place, middle, 0, size), middle)
    yield


def exchange_kernel(
    width,
    depth,
    split,
    total_ref,
    dense_ref,
    all_ref,
    coadd_ref,
    held_ref,
    az_ref,
    az_half,
    ax_ref,
    ax_half,
    bx_ref,
    bx_half,
    bz_ref,
    bz_half,
    send_ref,
    recv_ref,
):
    rows = dense_ref.shape[3]
    band = coadd_ref.shape[0]
    me = lax.axis_index("det")
    core = lax.rem(me, 2)
    z = lax.rem(me // 2, depth)
    x = me // (2 * depth)
    other = {"det": det_index(x, z, 1 - core, depth)}
    beside = [{"det": det_index(signed(x, 1, way, width), z, core, depth)} for way in (0, 1)]
    along = [{"det": det_index(x, signed(z, 1, way, depth), core, depth)} for way in (0, 1)]
    barrier = pltpu.get_barrier_semaphore()
    friends = [other] + beside + along
    for friend in friends:
        pl.semaphore_signal(barrier, inc=1, device_id=friend, device_id_type=pl.DeviceIdType.MESH)
    pl.semaphore_wait(barrier, len(friends))

    links = Links(send_ref, recv_ref)
    rest = rows - split

    def everything(l, size):
        return pl.ds(0, size) if l is None else l

    def a_at(dest, l, lo, length):
        return (everything(l, width), dest, pl.ds(lo, length), slice(None))

    def b_at(dest, l, lo, length):
        return (dest, everything(l, depth), pl.ds(split + lo, length), slice(None))

    def a_next(dest, l, lo, length):
        return (pl.ds(dest, 1) if l is None else dest, z, pl.ds(lo, length), slice(None))

    def b_next(dest, l, lo, length):
        return (pl.ds(x, 1) if l is None else x, dest, pl.ds(split + lo, length), slice(None))

    def with_core(index, which):
        return index[:2] + (which,) + index[2:]

    def hand_over(tag, dest, at, length):
        index = at(dest, None, 0, length)
        links.start(tag, dense_ref.at[with_core(index, 1 - core)], held_ref.at[index], other)

    zs = [(depth // 2, 0)] + [(s, w) for s in range(depth // 2 - 1, 0, -1) for w in (0, 1)] + [(0, 0)]
    xs = [(width // 2, 0)] + [(s, w) for s in range(width // 2 - 1, 0, -1) for w in (0, 1)] + [(0, 0)]
    turns = [("b", xs[0]), ("a", zs[0]), ("a", zs[1]), ("a", zs[2])]
    turns += [("b", k) for k in xs[1:-1]] + [("a", k) for k in zs[3:]] + [("b", xs[-1])]
    for part, (step, way) in turns:
        if part == "a":
            hand_over(("core a", step, way), signed(z, step, way, depth), a_at, split)
        else:
            hand_over(("core b", step, way), signed(x, step, way, width), b_at, rest)

    def base_of(tag, order, at):
        left = list(order)

        def base(dest):
            step, way = left.pop(0)
            links.arrive((tag, step, way))

        base.ref = dense_ref
        base.index = lambda *key: with_core(at(*key), core)
        return base

    def divided(offset):
        def store(l, lo, index, total):
            start, end = offset + lo, offset + lo + total.shape[0]
            while start < end:
                box = start // band
                stop = min(end, (box + 1) * band)
                part = total[start - offset - lo : stop - offset - lo] / jnp.maximum(total_ref[box], 1.0)
                part = part.astype(jnp.bfloat16)
                all_ref[x, z, core, pl.ds(start, stop - start), :] = part
                coadd_ref[pl.ds(start - box * band, stop - start), pl.ds(box * TILE, TILE)] = part
                start = stop

        return store

    a_first = ring_reduce(
        links, "a z", depth, z, width, split, a_at, held_ref, az_ref, az_half, lambda w: along[w],
        base_of("core a", zs, a_at), None,
    )
    b_first = ring_reduce(
        links, "b x", width, x, depth, rest, b_at, held_ref, bx_ref, bx_half, lambda w: beside[w],
        base_of("core b", xs, b_at), None,
    )
    a_second = ring_reduce(
        links, "a x", width, x, 1, split, a_next, held_ref, ax_ref, ax_half, lambda w: beside[w], None, divided(0)
    )
    b_second = ring_reduce(
        links, "b z", depth, z, 1, rest, b_next, held_ref, bz_ref, bz_half, lambda w: along[w], None, divided(split)
    )

    def a_view(origin, lo, length):
        return all_ref.at[:, origin, core, pl.ds(lo, length), :]

    def b_view(origin, lo, length):
        return all_ref.at[origin, :, core, pl.ds(split + lo, length), :]

    def a_own(origin, lo, length):
        return all_ref.at[origin, z, core, pl.ds(lo, length), :]

    def b_own(origin, lo, length):
        return all_ref.at[x, origin, core, pl.ds(split + lo, length), :]

    def nothing(origin, key):
        return None

    def across(tag, view, length):
        def arrived(origin, key):
            links.start((tag, key), view(origin, 0, length), view(origin, 0, length), other)

        return arrived

    a_third = ring_gather(links, "a gather x", width, x, split, a_own, lambda w: beside[w], nothing)
    b_third = ring_gather(links, "b gather z", depth, z, rest, b_own, lambda w: along[w], nothing)
    a_last = ring_gather(
        links, "a gather z", depth, z, split, a_view, lambda w: along[w], across("core a back", a_view, split)
    )
    b_last = ring_gather(
        links, "b gather x", width, x, rest, b_view, lambda w: beside[w], across("core b back", b_view, rest)
    )

    def chain(*parts):
        for part in parts:
            yield from part

    a_run = chain(a_first, a_second, a_third, a_last)
    b_run = chain(b_first, b_second, b_third, b_last)
    order = "ba" "a" "b" "aa" "ba" "baba" "bab" "bab" "abab" "b" "aabaabaab"
    runs = {"a": a_run, "b": b_run}
    for name in order:
        next(runs[name], None)
    for run in runs.values():
        for _ in run:
            pass
    for key in list(links.copies):
        if key[0] in ("core a back", "core b back"):
            links.arrive(key)
    links.finish()


def exchange(totals, dense, width, depth, split):
    rows = dense.shape[3]
    band = rows // totals.shape[0]
    rest = rows - split
    copies = 2 * (2 * width + 2 * depth + 4) + 16

    def buffers(size, lead, length):
        return [
            pltpu.VMEM((size // 2 - 1, 2, lead, length, TILE), jnp.bfloat16),
            pltpu.VMEM((2, lead, length // 2, TILE), jnp.bfloat16),
        ]

    return pl.pallas_call(
        functools.partial(exchange_kernel, width, depth, split),
        in_specs=[pl.BlockSpec(memory_space=pltpu.SMEM), pl.BlockSpec(memory_space=pltpu.VMEM)],
        out_specs=[pl.BlockSpec(memory_space=pltpu.VMEM)] * 2,
        out_shape=[
            jax.ShapeDtypeStruct(dense.shape, jnp.bfloat16),
            jax.ShapeDtypeStruct((band, totals.shape[0] * TILE), jnp.bfloat16),
        ],
        scratch_shapes=[pltpu.VMEM((width, depth, rows, TILE), jnp.bfloat16)]
        + buffers(depth, width, split)
        + buffers(width, 1, split)
        + buffers(width, depth, rest)
        + buffers(depth, 1, rest)
        + [pltpu.SemaphoreType.DMA((copies,)), pltpu.SemaphoreType.DMA((copies,))],
        compiler_params=pltpu.CompilerParams(
            collective_id=0, has_side_effects=True, vmem_limit_bytes=40 << 20
        ),
        name="exchange",
    )(totals, dense)


def base_rows(psf_coef, taps):
    images = psf_coef.shape[0]
    kernels, span = taps.shape
    scaled = (psf_coef[:, :, None] * taps[None]).astype(jnp.bfloat16)
    by_tap = jnp.transpose(scaled, (0, 2, 1))
    lead = jnp.pad(by_tap, ((0, 0), (0, 1), (0, 0)))
    late = jnp.pad(by_tap, ((0, 0), (1, 0), (0, 0)))
    both = jnp.concatenate([lead, late], axis=2)
    lanes = jnp.arange(TILE)[None, :]
    taken = jnp.arange(span)[:, None]
    here = ((-taken) % TILE == lanes).astype(jnp.float32)
    there = (HALF - taken == lanes).astype(jnp.float32)
    half = taps.astype(jnp.bfloat16).astype(jnp.float32)
    placed = jnp.concatenate(
        [
            jnp.dot(half, here, precision=lax.Precision.HIGHEST),
            jnp.dot(half, there, precision=lax.Precision.HIGHEST),
        ],
        axis=0,
    ).astype(jnp.bfloat16)
    return jnp.einsum("itk,kc->itc", both, placed, preferred_element_type=jnp.float32)


def per_device(
    images,
    warp_rows,
    warp_cols,
    psf_coef,
    taps,
    dest_patch,
    dest_block,
    weight_index,
    weight_table,
    patch_home,
):
    dets, visits, band, cols = images.shape
    reach = (taps.shape[1] - 1) // 2
    tiles = cols // TILE
    count = dets * visits
    patches = patch_home.shape[0]
    me = lax.axis_index("det")
    row_size = lax.axis_size("row")

    rows = warp_rows.reshape(count, band, cols)
    up = [(i, i + 1) for i in range(row_size - 1)]
    down = [(j, i) for i, j in up]
    before = lax.ppermute(rows[:, band - HALO :], "row", up)
    after = lax.ppermute(rows[:, :HALO], "row", down)
    rows_ext = jnp.concatenate([before, rows, after], axis=1)
    col_warped = jnp.einsum(
        "nbs,nst->nbt",
        images.reshape(count, band, cols),
        warp_cols.reshape(count, cols, cols),
        preferred_element_type=jnp.float32,
    ).astype(jnp.bfloat16)
    full = lax.all_gather(col_warped, "row", axis=1, tiled=True)

    base = base_rows(psf_coef.reshape(count, -1), taps)
    matched = match(base, rows_ext, full, reach)

    levels = weight_table.shape[0]
    flat_index = weight_index.reshape(-1)
    weight_all = jnp.sum(
        jnp.where(flat_index[:, None] == jnp.arange(levels)[None, :], weight_table[None, :], 0.0), axis=1
    )
    weight_mine = lax.dynamic_slice_in_dim(weight_all, me * count, count, 0)
    patch_mine = lax.dynamic_slice_in_dim(dest_patch[:, 0], me * count * tiles, count * tiles, 0)
    block_mine = lax.dynamic_slice_in_dim(dest_block, me * count * tiles, count * tiles, 0)
    home_mine = jnp.sum(
        jnp.where(patch_mine[:, None] == jnp.arange(patches)[None, :], patch_home[None, :], 0), axis=1
    )
    targets = home_mine * tiles + block_mine
    my_patch = jnp.sum(jnp.where(patch_home == me, jnp.arange(patches), 0))
    to_mine = jnp.where(dest_patch[:, 0] == my_patch, dest_block, -1).reshape(-1, tiles)
    denominator = jnp.stack(
        [jnp.sum(jnp.where(to_mine == b, weight_all[:, None], 0.0)) for b in range(tiles)]
    )

    dense = collect(targets, weight_mine, matched, patches * tiles)
    depth = DEPTH
    width = patches // (2 * depth)
    shape = (width, depth, 2, tiles * band, TILE)
    templates, coadd = exchange(denominator, dense.reshape(shape), width, depth, SPLIT)
    templates = templates.reshape(patches * tiles, band, TILE)
    difference = subtract(targets, matched, templates)
    return (difference.reshape(dets, visits, band, cols), coadd[None])


def solution(mesh):
    placed = (
        P("det", None, "row", None),
        P("det", None, "row", None),
        P("det", None, None, None),
        P("det", None, None),
        P(),
        P(),
        P(),
        P(),
        P(),
        P(),
    )
    return jax.shard_map(
        per_device,
        mesh=mesh,
        in_specs=placed,
        out_specs=(P("det", None, "row", None), P("det", "row", None)),
        check_vma=False,
    )
```

```python
import functools

import jax
import jax.numpy as jnp
from jax import lax
from jax.experimental import pallas as pl
from jax.experimental.pallas import tpu as pltpu
from jax.sharding import PartitionSpec as P

TILE = 128
HALF = 64
HALO = 16
GROUP = 4
DEPTH = 8
SPLIT = 128
PASS_ON = 2
LAG = 4


def build_table(base_ref, image, keep, table_ref, offsets):
    for t in range(offsets - 2):
        row = jnp.broadcast_to(base_ref[image, pl.ds(t, 1), :], keep.shape)
        band = pltpu.roll(row, 0, 1, stride=1, stride_axis=0)
        band = jnp.where(keep, band, 0.0).astype(jnp.bfloat16)
        table_ref[pl.ds(t * TILE, keep.shape[0]), pl.ds(0, TILE)] = band
        table_ref[pl.ds((t + 2) * TILE, keep.shape[0]), pl.ds(TILE, TILE)] = band


def table_mask(span):
    rows = lax.broadcasted_iota(jnp.int32, (96, TILE), 0)
    lanes = lax.broadcasted_iota(jnp.int32, (96, TILE), 1)
    gap = rows - jnp.where(lanes >= HALF, lanes - HALF, lanes)
    return (gap >= 0) & (gap < span)


def convolve(warped, reach, window_ref, left_ref, table_ref, out_ref, image, offsets):
    rows, cols = warped.shape
    wide = jnp.concatenate([warped, jnp.zeros((rows, TILE), jnp.float32)], axis=1)
    even = pltpu.roll(wide, reach, 1)
    odd = pltpu.roll(wide, cols + TILE + reach - HALF, 1)
    tiles = cols // TILE
    groups = out_ref.shape[2] // GROUP
    for tile in range(tiles):
        window_ref[2 * tile] = even[:, tile * TILE : (tile + 1) * TILE]
        window_ref[2 * tile + 1] = odd[:, tile * TILE : (tile + 1) * TILE]
    for offset in range(offsets):
        start = HALO - reach + offset
        parts = [window_ref[w, pl.ds(start, groups, stride=GROUP), :] for w in range(2 * tiles)]
        left_ref[:, pl.ds(offset * TILE, TILE)] = jnp.concatenate(parts, axis=0).astype(jnp.bfloat16)
    product = jnp.dot(left_ref[...], table_ref[...], preferred_element_type=jnp.float32)
    low = lax.broadcasted_iota(jnp.int32, (groups, TILE), 1) < HALF
    for tile in range(tiles):
        for pair in range(2):
            first = product[(2 * tile) * groups : (2 * tile + 1) * groups, pair * TILE : (pair + 1) * TILE]
            second = product[(2 * tile + 1) * groups : (2 * tile + 2) * groups, pair * TILE : (pair + 1) * TILE]
            upper = jnp.where(low, first, pltpu.roll(second, HALF, 1))
            lower = jnp.where(low, pltpu.roll(first, HALF, 1), second)
            out_ref[image, tile, pl.ds(2 * pair, groups, stride=GROUP), :] = upper
            out_ref[image, tile, pl.ds(2 * pair + 1, groups, stride=GROUP), :] = lower


def collect_kernel(tiles, target_ref, weight_ref, matched_ref, dense_ref):
    image = pl.program_id(0)

    @pl.when(image == 0)
    def _():
        dense_ref[...] = jnp.zeros_like(dense_ref)

    for tile in range(tiles):
        piece = weight_ref[image] * matched_ref[image, tile]
        piece = piece.astype(jnp.bfloat16).astype(jnp.float32)
        target = target_ref[image * tiles + tile]
        dense_ref[target] = (dense_ref[target].astype(jnp.float32) + piece).astype(jnp.bfloat16)


def collect(targets, weights, matched, boxes):
    images, tiles, band, _ = matched.shape
    return pl.pallas_call(
        functools.partial(collect_kernel, tiles),
        grid_spec=pltpu.PrefetchScalarGridSpec(
            num_scalar_prefetch=2,
            grid=(images,),
            in_specs=[pl.BlockSpec(memory_space=pltpu.VMEM)],
            out_specs=pl.BlockSpec((boxes, band, TILE), lambda i, *_: (0, 0, 0), pipeline_mode=pl.Buffered(1)),
        ),
        out_shape=jax.ShapeDtypeStruct((boxes, band, TILE), jnp.bfloat16),
        compiler_params=pltpu.CompilerParams(vmem_limit_bytes=32 << 20),
        name="collect",
    )(targets, weights, matched)


def subtract_kernel(tiles, target_ref, matched_ref, template_ref, out_ref):
    image = pl.program_id(0)
    for tile in range(tiles):
        target = target_ref[image * tiles + tile]
        lanes = pl.ds(tile * TILE, TILE)
        out_ref[0, :, lanes] = (matched_ref[image, tile] - template_ref[target].astype(jnp.float32)).astype(jnp.bfloat16)


def subtract(targets, matched, templates):
    images, tiles, band, _ = matched.shape
    return pl.pallas_call(
        functools.partial(subtract_kernel, tiles),
        grid_spec=pltpu.PrefetchScalarGridSpec(
            num_scalar_prefetch=1,
            grid=(images,),
            in_specs=[
                pl.BlockSpec(memory_space=pltpu.VMEM),
                pl.BlockSpec(memory_space=pltpu.VMEM),
            ],
            out_specs=pl.BlockSpec((1, band, tiles * TILE), lambda i, *_: (i, 0, 0)),
        ),
        out_shape=jax.ShapeDtypeStruct((images, band, tiles * TILE), jnp.bfloat16),
        compiler_params=pltpu.CompilerParams(vmem_limit_bytes=32 << 20),
        name="subtract",
    )(targets, matched, templates)


def det_index(x, z, core, depth):
    return (x * depth + z) * 2 + core


class Links:
    def __init__(self, send_ref, recv_ref):
        self.send_ref, self.recv_ref = send_ref, recv_ref
        self.copies = {}

    def start(self, key, source, target, device):
        index = len(self.copies)
        copy = pltpu.make_async_remote_copy(
            src_ref=source,
            dst_ref=target,
            send_sem=self.send_ref.at[index],
            recv_sem=self.recv_ref.at[index],
            device_id=device,
            device_id_type=pl.DeviceIdType.MESH,
        )
        copy.start()
        self.copies[key] = copy

    def arrive(self, key):
        self.copies[key].wait_recv()

    def finish(self):
        for copy in self.copies.values():
            copy.wait_send()


def signed(place, step, way, size):
    return lax.rem(place + size + (step if way == 0 else -step), size)


def ring_reduce(links, tag, size, place, lead, rows, at, held_ref, whole_ref, half_ref, neighbour, base, finish):
    middle, half = size // 2, rows // 2

    def add(dest, extras, store):
        if base is not None:
            base(dest)

        def body(l, carry):
            for lo in (0, half):
                index = at(dest, l, lo, half)
                total = held_ref[index].astype(jnp.float32)
                if base is not None:
                    total = total + base.ref[base.index(dest, l, lo, half)].astype(jnp.float32)
                for ref, way, from_half in extras:
                    if not from_half:
                        total = total + ref[way, l, pl.ds(lo, half), :].astype(jnp.float32)
                    elif lo == way * half:
                        total = total + ref[way, l].astype(jnp.float32)
                store(l, lo, index, total)
            return carry

        lax.fori_loop(0, lead, body, 0)

    def put(l, lo, index, total):
        held_ref[index] = total.astype(jnp.bfloat16)

    far = signed(place, middle, 0, size)
    if base is not None:
        add(far, [], put)
    for way in (0, 1):
        links.start((tag, way, middle), held_ref.at[at(far, None, way * half, half)], half_ref.at[way], neighbour(way))
    yield
    for step in range(middle - 1, 0, -1):
        for way in (0, 1):
            dest = signed(place, step, way, size)
            links.arrive((tag, way, step + 1))
            source = (half_ref, way, True) if step + 1 == middle else (whole_ref.at[step], way, False)
            add(dest, [source], put)
            links.start(
                (tag, way, step), held_ref.at[at(dest, None, 0, rows)], whole_ref.at[step - 1, way], neighbour(way)
            )
        yield
    for way in (0, 1):
        links.arrive((tag, way, 1))
    add(place, [(whole_ref.at[0], 0, False), (whole_ref.at[0], 1, False)], put if finish is None else finish)
    yield


def ring_gather(links, tag, size, place, rows, view, neighbour, arrived):
    middle, half = size // 2, rows // 2
    for way in (0, 1):
        links.start((tag, way, 1), view(place, 0, rows), view(place, 0, rows), neighbour(way))
    arrived(place, 0)
    yield
    for step in range(1, middle):
        for way in (0, 1):
            origin = signed(place, step, 1 - way, size)
            links.arrive((tag, way, step))
            lo, length = (0, rows) if step + 1 < middle else (way * half, half)
            links.start((tag, way, step + 1), view(origin, lo, length), view(origin, lo, length), neighbour(way))
            arrived(origin, (step, way))
        yield
    for way in (0, 1):
        links.arrive((tag, way, middle))
    arrived(signed(place, middle, 0, size), middle)
    yield


def exchange_kernel(
    width,
    depth,
    split,
    total_ref,
    dense_ref,
    all_ref,
    coadd_ref,
    held_ref,
    az_ref,
    az_half,
    ax_ref,
    ax_half,
    bx_ref,
    bx_half,
    bz_ref,
    bz_half,
    send_ref,
    recv_ref,
):
    rows = dense_ref.shape[3]
    band = coadd_ref.shape[0]
    me = lax.axis_index("det")
    core = lax.rem(me, 2)
    z = lax.rem(me // 2, depth)
    x = me // (2 * depth)
    other = {"det": det_index(x, z, 1 - core, depth)}
    beside = [{"det": det_index(signed(x, 1, way, width), z, core, depth)} for way in (0, 1)]
    along = [{"det": det_index(x, signed(z, 1, way, depth), core, depth)} for way in (0, 1)]
    barrier = pltpu.get_barrier_semaphore()
    friends = [other] + beside + along
    for friend in friends:
        pl.semaphore_signal(barrier, inc=1, device_id=friend, device_id_type=pl.DeviceIdType.MESH)
    pl.semaphore_wait(barrier, len(friends))

    links = Links(send_ref, recv_ref)
    rest = rows - split

    def everything(l, size):
        return pl.ds(0, size) if l is None else l

    def a_at(dest, l, lo, length):
        return (everything(l, width), dest, pl.ds(lo, length), slice(None))

    def b_at(dest, l, lo, length):
        return (dest, everything(l, depth), pl.ds(split + lo, length), slice(None))

    def a_next(dest, l, lo, length):
        return (pl.ds(dest, 1) if l is None else dest, z, pl.ds(lo, length), slice(None))

    def b_next(dest, l, lo, length):
        return (pl.ds(x, 1) if l is None else x, dest, pl.ds(split + lo, length), slice(None))

    def with_core(index, which):
        return index[:2] + (which,) + index[2:]

    def hand_over(tag, dest, at, length):
        index = at(dest, None, 0, length)
        links.start(tag, dense_ref.at[with_core(index, 1 - core)], held_ref.at[index], other)

    zs = [(depth // 2, 0)] + [(s, w) for s in range(depth // 2 - 1, 0, -1) for w in (0, 1)] + [(0, 0)]
    xs = [(width // 2, 0)] + [(s, w) for s in range(width // 2 - 1, 0, -1) for w in (0, 1)] + [(0, 0)]
    turns = [("b", xs[0]), ("a", zs[0]), ("a", zs[1]), ("a", zs[2])]
    turns += [("b", k) for k in xs[1:-1]] + [("a", k) for k in zs[3:]] + [("b", xs[-1])]
    for part, (step, way) in turns:
        if part == "a":
            hand_over(("core a", step, way), signed(z, step, way, depth), a_at, split)
        else:
            hand_over(("core b", step, way), signed(x, step, way, width), b_at, rest)

    def base_of(tag, order, at):
        left = list(order)

        def base(dest):
            step, way = left.pop(0)
            links.arrive((tag, step, way))

        base.ref = dense_ref
        base.index = lambda *key: with_core(at(*key), core)
        return base

    def divided(offset):
        def store(l, lo, index, total):
            start, end = offset + lo, offset + lo + total.shape[0]
            while start < end:
                box = start // band
                stop = min(end, (box + 1) * band)
                part = total[start - offset - lo : stop - offset - lo] / jnp.maximum(total_ref[box], 1.0)
                part = part.astype(jnp.bfloat16)
                all_ref[x, z, core, pl.ds(start, stop - start), :] = part
                coadd_ref[pl.ds(start - box * band, stop - start), pl.ds(box * TILE, TILE)] = part
                start = stop

        return store

    a_first = ring_reduce(
        links, "a z", depth, z, width, split, a_at, held_ref, az_ref, az_half, lambda w: along[w],
        base_of("core a", zs, a_at), None,
    )
    b_first = ring_reduce(
        links, "b x", width, x, depth, rest, b_at, held_ref, bx_ref, bx_half, lambda w: beside[w],
        base_of("core b", xs, b_at), None,
    )
    a_second = ring_reduce(
        links, "a x", width, x, 1, split, a_next, held_ref, ax_ref, ax_half, lambda w: beside[w], None, divided(0)
    )
    b_second = ring_reduce(
        links, "b z", depth, z, 1, rest, b_next, held_ref, bz_ref, bz_half, lambda w: along[w], None, divided(split)
    )

    def a_view(origin, lo, length):
        return all_ref.at[:, origin, core, pl.ds(lo, length), :]

    def b_view(origin, lo, length):
        return all_ref.at[origin, :, core, pl.ds(split + lo, length), :]

    def a_own(origin, lo, length):
        return all_ref.at[origin, z, core, pl.ds(lo, length), :]

    def b_own(origin, lo, length):
        return all_ref.at[x, origin, core, pl.ds(split + lo, length), :]

    def nothing(origin, key):
        return None

    def across(tag, view, length):
        def arrived(origin, key):
            links.start((tag, key), view(origin, 0, length), view(origin, 0, length), other)

        return arrived

    a_third = ring_gather(links, "a gather x", width, x, split, a_own, lambda w: beside[w], nothing)
    b_third = ring_gather(links, "b gather z", depth, z, rest, b_own, lambda w: along[w], nothing)
    a_last = ring_gather(
        links, "a gather z", depth, z, split, a_view, lambda w: along[w], across("core a back", a_view, split)
    )
    b_last = ring_gather(
        links, "b gather x", width, x, rest, b_view, lambda w: beside[w], across("core b back", b_view, rest)
    )

    def chain(*parts):
        for part in parts:
            yield from part

    a_run = chain(a_first, a_second, a_third, a_last)
    b_run = chain(b_first, b_second, b_third, b_last)
    order = "ba" "a" "b" "aa" "ba" "baba" "bab" "bab" "abab" "b" "aabaabaab"
    runs = {"a": a_run, "b": b_run}
    for name in order:
        next(runs[name], None)
    for run in runs.values():
        for _ in run:
            pass
    for key in list(links.copies):
        if key[0] in ("core a back", "core b back"):
            links.arrive(key)
    links.finish()


def exchange(totals, dense, width, depth, split):
    rows = dense.shape[3]
    band = rows // totals.shape[0]
    rest = rows - split
    copies = 2 * (2 * width + 2 * depth + 4) + 16

    def buffers(size, lead, length):
        return [
            pltpu.VMEM((size // 2 - 1, 2, lead, length, TILE), jnp.bfloat16),
            pltpu.VMEM((2, lead, length // 2, TILE), jnp.bfloat16),
        ]

    return pl.pallas_call(
        functools.partial(exchange_kernel, width, depth, split),
        in_specs=[pl.BlockSpec(memory_space=pltpu.SMEM), pl.BlockSpec(memory_space=pltpu.VMEM)],
        out_specs=[pl.BlockSpec(memory_space=pltpu.VMEM)] * 2,
        out_shape=[
            jax.ShapeDtypeStruct(dense.shape, jnp.bfloat16),
            jax.ShapeDtypeStruct((band, totals.shape[0] * TILE), jnp.bfloat16),
        ],
        scratch_shapes=[pltpu.VMEM((width, depth, rows, TILE), jnp.bfloat16)]
        + buffers(depth, width, split)
        + buffers(width, 1, split)
        + buffers(width, depth, rest)
        + buffers(depth, 1, rest)
        + [pltpu.SemaphoreType.DMA((copies,)), pltpu.SemaphoreType.DMA((copies,))],
        compiler_params=pltpu.CompilerParams(
            collective_id=0, has_side_effects=True, vmem_limit_bytes=40 << 20
        ),
        name="exchange",
    )(totals, dense)


def gather_match_kernel(
    reach,
    offsets,
    base_ref,
    images_hbm,
    rows_hbm,
    cols_hbm,
    out_ref,
    images_ref,
    rows_ref,
    cols_ref,
    full_ref,
    halo_ref,
    window_ref,
    left_ref,
    table_ref,
    load_ref,
    send_ref,
    recv_ref,
):
    count, band, side = images_hbm.shape
    half = band // 2
    size = full_ref.shape[1]
    me = lax.axis_index("row")
    beside = [signed(me, 1, way, size) for way in (0, 1)]

    def local(kind, image):
        source, target = ((images_hbm, images_ref), (cols_hbm, cols_ref), (rows_hbm, rows_ref))[kind]
        return pltpu.make_async_copy(source.at[image], target.at[image], load_ref.at[kind, image])

    def remote(kind, image, source, target, way):
        return pltpu.make_async_remote_copy(
            src_ref=source,
            dst_ref=target,
            send_sem=send_ref.at[kind, image],
            recv_sem=recv_ref.at[kind, image],
            device_id={"row": beside[way]},
            device_id_type=pl.DeviceIdType.MESH,
        )

    def own(image, way):
        place = full_ref.at[image, me]
        return remote(way, image, place, place, way)

    def forward(image, way):
        place = full_ref.at[image, beside[1 - way], pl.ds(way * half, half), :]
        return remote(2 + way, image, place, place, way)

    def edge(image, way):
        start = band - HALO if way == 0 else 0
        return remote(4 + way, image, rows_hbm.at[image, pl.ds(start, HALO), :], halo_ref.at[image, way], way)

    for kind in range(3):
        @pl.loop(0, count)
        def _(image):
            local(kind, image).start()

    barrier = pltpu.get_barrier_semaphore()
    for friend in beside:
        pl.semaphore_signal(barrier, inc=1, device_id={"row": friend}, device_id_type=pl.DeviceIdType.MESH)
    table_ref[...] = jnp.zeros_like(table_ref)
    keep = table_mask(2 * reach + 1)
    first = jnp.where(me == 0, 0.0, 1.0)
    last = jnp.where(me == size - 1, 0.0, 1.0)
    pl.semaphore_wait(barrier, 2)

    @pl.loop(0, count + LAG)
    def _(step):
        @pl.when(step < count)
        def _():
            local(0, step).wait()
            local(1, step).wait()
            mapped = jnp.dot(images_ref[step], cols_ref[step], preferred_element_type=jnp.float32)
            full_ref[step, me] = mapped.astype(jnp.bfloat16)
            for way in (0, 1):
                own(step, way).start()
                edge(step, way).start()

        @pl.when((step >= PASS_ON) & (step < count + PASS_ON))
        def _():
            image = step - PASS_ON
            for way in (0, 1):
                own(image, way).wait_recv()
                forward(image, way).start()

        @pl.when(step >= LAG)
        def _():
            image = step - LAG
            build_table(base_ref, image, keep, table_ref, offsets)
            local(2, image).wait()
            for way in (0, 1):
                forward(image, way).wait_recv()
                edge(image, way).wait_recv()
            rows = jnp.concatenate([halo_ref[image, 0], rows_ref[image], halo_ref[image, 1]], axis=0)
            full = full_ref[image].reshape(side, side)
            warped = jnp.dot(rows, full, preferred_element_type=jnp.float32)
            warped = jnp.concatenate(
                [warped[:HALO] * first, warped[HALO : HALO + band], warped[HALO + band :] * last], axis=0
            )
            convolve(warped, reach, window_ref, left_ref, table_ref, out_ref, image, offsets)

    @pl.loop(0, count)
    def _(image):
        for way in (0, 1):
            own(image, way).wait_send()
            forward(image, way).wait_send()
            edge(image, way).wait_send()


def gather_match(base, images, rows, cols, size, reach):
    count, band, side = images.shape
    offsets = 2 * reach + GROUP
    tiles = side // TILE
    hbm = pl.BlockSpec(memory_space=pl.ANY)
    return pl.pallas_call(
        functools.partial(gather_match_kernel, reach, offsets),
        in_specs=[pl.BlockSpec(memory_space=pltpu.VMEM), hbm, hbm, hbm],
        out_specs=pl.BlockSpec(memory_space=pltpu.VMEM),
        out_shape=jax.ShapeDtypeStruct((count, tiles, band, TILE), jnp.float32),
        scratch_shapes=[
            pltpu.VMEM((count, band, side), jnp.bfloat16),
            pltpu.VMEM((count, band, side), jnp.bfloat16),
            pltpu.VMEM((count, side, side), jnp.bfloat16),
            pltpu.VMEM((count, size, band, side), jnp.bfloat16),
            pltpu.VMEM((count, 2, HALO, side), jnp.bfloat16),
            pltpu.VMEM((2 * tiles, band + 2 * HALO, TILE), jnp.float32),
            pltpu.VMEM((2 * tiles * (band // GROUP), offsets * TILE), jnp.bfloat16),
            pltpu.VMEM((offsets * TILE, 2 * TILE), jnp.bfloat16),
            pltpu.SemaphoreType.DMA((3, count)),
            pltpu.SemaphoreType.DMA((6, count)),
            pltpu.SemaphoreType.DMA((6, count)),
        ],
        compiler_params=pltpu.CompilerParams(
            collective_id=1, has_side_effects=True, vmem_limit_bytes=40 << 20
        ),
        name="gather_match",
    )(base, images, rows, cols)


def base_rows(psf_coef, taps):
    images = psf_coef.shape[0]
    kernels, span = taps.shape
    scaled = (psf_coef[:, :, None] * taps[None]).astype(jnp.bfloat16)
    by_tap = jnp.transpose(scaled, (0, 2, 1))
    lead = jnp.pad(by_tap, ((0, 0), (0, 1), (0, 0)))
    late = jnp.pad(by_tap, ((0, 0), (1, 0), (0, 0)))
    both = jnp.concatenate([lead, late], axis=2)
    lanes = jnp.arange(TILE)[None, :]
    taken = jnp.arange(span)[:, None]
    here = ((-taken) % TILE == lanes).astype(jnp.float32)
    there = (HALF - taken == lanes).astype(jnp.float32)
    half = taps.astype(jnp.bfloat16).astype(jnp.float32)
    placed = jnp.concatenate(
        [
            jnp.dot(half, here, precision=lax.Precision.HIGHEST),
            jnp.dot(half, there, precision=lax.Precision.HIGHEST),
        ],
        axis=0,
    ).astype(jnp.bfloat16)
    return jnp.einsum("itk,kc->itc", both, placed, preferred_element_type=jnp.float32)


def per_device(
    images,
    warp_rows,
    warp_cols,
    psf_coef,
    taps,
    dest_patch,
    dest_block,
    weight_index,
    weight_table,
    patch_home,
):
    dets, visits, band, cols = images.shape
    reach = (taps.shape[1] - 1) // 2
    tiles = cols // TILE
    count = dets * visits
    patches = patch_home.shape[0]
    me = lax.axis_index("det")
    row_size = lax.axis_size("row")

    base = base_rows(psf_coef.reshape(count, -1), taps)
    matched = gather_match(
        base,
        images.reshape(count, band, cols),
        warp_rows.reshape(count, band, cols),
        warp_cols.reshape(count, cols, cols),
        row_size,
        reach,
    )

    levels = weight_table.shape[0]
    flat_index = weight_index.reshape(-1)
    weight_all = jnp.sum(
        jnp.where(flat_index[:, None] == jnp.arange(levels)[None, :], weight_table[None, :], 0.0), axis=1
    )
    weight_mine = lax.dynamic_slice_in_dim(weight_all, me * count, count, 0)
    patch_mine = lax.dynamic_slice_in_dim(dest_patch[:, 0], me * count * tiles, count * tiles, 0)
    block_mine = lax.dynamic_slice_in_dim(dest_block, me * count * tiles, count * tiles, 0)
    home_mine = jnp.sum(
        jnp.where(patch_mine[:, None] == jnp.arange(patches)[None, :], patch_home[None, :], 0), axis=1
    )
    targets = home_mine * tiles + block_mine
    my_patch = jnp.sum(jnp.where(patch_home == me, jnp.arange(patches), 0))
    to_mine = jnp.where(dest_patch[:, 0] == my_patch, dest_block, -1).reshape(-1, tiles)
    denominator = jnp.stack(
        [jnp.sum(jnp.where(to_mine == b, weight_all[:, None], 0.0)) for b in range(tiles)]
    )

    dense = collect(targets, weight_mine, matched, patches * tiles)
    depth = DEPTH
    width = patches // (2 * depth)
    shape = (width, depth, 2, tiles * band, TILE)
    templates, coadd = exchange(denominator, dense.reshape(shape), width, depth, SPLIT)
    templates = templates.reshape(patches * tiles, band, TILE)
    difference = subtract(targets, matched, templates)
    return (difference.reshape(dets, visits, band, cols), coadd[None])


def solution(mesh):
    placed = (
        P("det", None, "row", None),
        P("det", None, "row", None),
        P("det", None, None, None),
        P("det", None, None),
        P(),
        P(),
        P(),
        P(),
        P(),
        P(),
    )
    return jax.shard_map(
        per_device,
        mesh=mesh,
        in_specs=placed,
        out_specs=(P("det", None, "row", None), P("det", "row", None)),
        check_vma=False,
    )
```

```python
import functools

import jax
import jax.numpy as jnp
from jax import lax
from jax.experimental import pallas as pl
from jax.experimental.pallas import tpu as pltpu
from jax.sharding import PartitionSpec as P

TILE = 128
HALF = 64
HALO = 16
GROUP = 4
DEPTH = 8
SPLIT = 128
PASS_ON = 2
LAG = 4
SUBTRACT_STEPS = 3


def one_hot(mask):
    return jnp.where(mask, 1.0, 0.0).astype(jnp.bfloat16)


def iota2(rows, cols, axis):
    return lax.broadcasted_iota(jnp.int32, (rows, cols), axis)


def tap_parts(taps, offsets):
    kernels, span = taps.shape
    shift = iota2(offsets, span, 0) - iota2(offsets, span, 1)

    def by_offset(late):
        pick = jnp.where(shift == late, 1.0, 0.0)
        return lax.dot_general(
            pick, taps, (((1,), (1,)), ((), ())), precision=lax.Precision.HIGHEST, preferred_element_type=jnp.float32
        )

    tap, lane = iota2(span, TILE, 0), iota2(span, TILE, 1)
    half = taps.astype(jnp.bfloat16)

    def placed(mask):
        return jnp.dot(half, one_hot(mask), preferred_element_type=jnp.float32).astype(jnp.bfloat16)

    here = placed((lane + tap == TILE) | ((tap == 0) & (lane == 0)))
    there = placed(lane + tap == HALF)
    return by_offset(0), by_offset(1), here, there


def base_rows(coef, parts):
    lead, late, here, there = parts
    left = jnp.dot((coef * lead).astype(jnp.bfloat16), here, preferred_element_type=jnp.float32)
    return left + jnp.dot((coef * late).astype(jnp.bfloat16), there, preferred_element_type=jnp.float32)


def denominators(patch_ref, block_ref, index_ref, table_ref, home_ref, out_ref, boxes):
    me = lax.axis_index("det")
    homes = home_ref[...]
    mine = jnp.sum(jnp.where(homes == me, iota2(1, homes.shape[1], 1), 0), axis=1, keepdims=True)
    visits, dets = index_ref.shape
    groups = dets // TILE
    period = visits * boxes
    row, lane = iota2(TILE, TILE, 0), iota2(TILE, TILE, 1)
    blank = jnp.zeros((8 - groups, TILE), jnp.float32)
    levels = []
    for visit in range(visits):
        parts = [index_ref[pl.ds(visit, 1), pl.ds(g * TILE, TILE)].astype(jnp.float32) for g in range(groups)]
        levels.append(jnp.concatenate(parts + [blank], axis=0).astype(jnp.bfloat16))
    sums = [jnp.zeros((groups, TILE), jnp.float32) for _ in range(boxes)]
    for k in range(period):
        level = jnp.zeros((8, TILE), jnp.float32)
        for visit in range(visits):
            gap = lane - period * row + (TILE * k - boxes * visit)
            level = level + jnp.dot(
                levels[visit], one_hot((gap >= 0) & (gap < boxes)), preferred_element_type=jnp.float32
            )
        level = level[:groups]
        weight = jnp.zeros((groups, TILE), jnp.float32)
        for n in range(table_ref.shape[0]):
            weight = jnp.where(level == float(n), table_ref[n], weight)
        patch = jnp.concatenate([patch_ref[pl.ds(g * period + k, 1), :] for g in range(groups)], axis=0)
        block = jnp.concatenate([block_ref[pl.ds(g * period + k, 1), :] for g in range(groups)], axis=0)
        for box in range(boxes):
            sums[box] = sums[box] + jnp.where((patch == mine) & (block == box), weight, 0.0)
    for box in range(boxes):
        total = jnp.sum(jnp.sum(sums[box], axis=0, keepdims=True), axis=1, keepdims=True)
        out_ref[pl.ds(box, 1), :] = jnp.broadcast_to(jnp.maximum(total, 1.0), (1, TILE))


def build_table(base, keep, table_ref, offsets):
    for t in range(offsets - 2):
        row = jnp.broadcast_to(base[t : t + 1], keep.shape)
        band = pltpu.roll(row, 0, 1, stride=1, stride_axis=0)
        band = jnp.where(keep, band, 0.0).astype(jnp.bfloat16)
        table_ref[pl.ds(t * TILE, keep.shape[0]), pl.ds(0, TILE)] = band
        table_ref[pl.ds((t + 2) * TILE, keep.shape[0]), pl.ds(TILE, TILE)] = band


def table_mask(span):
    rows = lax.broadcasted_iota(jnp.int32, (96, TILE), 0)
    lanes = lax.broadcasted_iota(jnp.int32, (96, TILE), 1)
    gap = rows - jnp.where(lanes >= HALF, lanes - HALF, lanes)
    return (gap >= 0) & (gap < span)


def convolve(warped, reach, window_ref, left_ref, table_ref, out_ref, image, offsets):
    rows, cols = warped.shape
    wide = jnp.concatenate([warped, jnp.zeros((rows, TILE), jnp.float32)], axis=1)
    even = pltpu.roll(wide, reach, 1)
    odd = pltpu.roll(wide, cols + TILE + reach - HALF, 1)
    tiles = cols // TILE
    groups = out_ref.shape[2] // GROUP
    for tile in range(tiles):
        window_ref[2 * tile] = even[:, tile * TILE : (tile + 1) * TILE]
        window_ref[2 * tile + 1] = odd[:, tile * TILE : (tile + 1) * TILE]
    for offset in range(offsets):
        start = HALO - reach + offset
        parts = [window_ref[w, pl.ds(start, groups, stride=GROUP), :] for w in range(2 * tiles)]
        left_ref[:, pl.ds(offset * TILE, TILE)] = jnp.concatenate(parts, axis=0).astype(jnp.bfloat16)
    product = jnp.dot(left_ref[...], table_ref[...], preferred_element_type=jnp.float32)
    low = lax.broadcasted_iota(jnp.int32, (groups, TILE), 1) < HALF
    for tile in range(tiles):
        for pair in range(2):
            first = product[(2 * tile) * groups : (2 * tile + 1) * groups, pair * TILE : (pair + 1) * TILE]
            second = product[(2 * tile + 1) * groups : (2 * tile + 2) * groups, pair * TILE : (pair + 1) * TILE]
            upper = jnp.where(low, first, pltpu.roll(second, HALF, 1))
            lower = jnp.where(low, pltpu.roll(first, HALF, 1), second)
            out_ref[image, tile, pl.ds(2 * pair, groups, stride=GROUP), :] = upper
            out_ref[image, tile, pl.ds(2 * pair + 1, groups, stride=GROUP), :] = lower


def collect_kernel(count, patch_ref, block_ref, index_ref, levels_ref, home_ref, matched_ref, dense_ref, target_ref):
    dets, tiles = count
    visits = index_ref.shape[0]
    me = lax.axis_index("det")
    dense_ref[...] = jnp.zeros_like(dense_ref)

    @pl.loop(0, dets)
    def _(det):
        for visit in range(visits):
            weight = levels_ref[index_ref[visit, me * dets + det]]
            for tile in range(tiles):
                local = (det * visits + visit) * tiles + tile
                piece = me * dets * visits * tiles + local
                row, lane = piece // TILE, lax.rem(piece, TILE)
                target = home_ref[patch_ref[row, lane]] * tiles + block_ref[row, lane]
                target_ref[local] = target
                value = (weight * matched_ref[det * visits + visit, tile]).astype(jnp.bfloat16)
                held = dense_ref[target].astype(jnp.float32)
                dense_ref[target] = (held + value.astype(jnp.float32)).astype(jnp.bfloat16)


def collect(patch, block, index, levels, home, matched, boxes):
    images, tiles, band, _ = matched.shape
    smem = pl.BlockSpec(memory_space=pltpu.SMEM)
    vmem = pl.BlockSpec(memory_space=pltpu.VMEM)
    return pl.pallas_call(
        functools.partial(collect_kernel, (images // index.shape[0], tiles)),
        in_specs=[smem] * 5 + [vmem],
        out_specs=[vmem, smem],
        out_shape=[
            jax.ShapeDtypeStruct((boxes, band, TILE), jnp.bfloat16),
            jax.ShapeDtypeStruct((images * tiles,), jnp.int32),
        ],
        compiler_params=pltpu.CompilerParams(vmem_limit_bytes=32 << 20),
        name="collect",
    )(patch, block, index, levels, home, matched)


def subtract_kernel(tiles, target_ref, matched_ref, template_ref, coadd_ref, out_ref, coadd_out):
    step = pl.program_id(0)
    images = out_ref.shape[0]

    @pl.when(step == 0)
    def _():
        coadd_out[...] = coadd_ref[...]

    @pl.loop(0, images)
    def _(local):
        image = step * images + local
        for tile in range(tiles):
            template = template_ref[target_ref[image * tiles + tile]].astype(jnp.float32)
            out_ref[local, :, pl.ds(tile * TILE, TILE)] = (matched_ref[image, tile] - template).astype(jnp.bfloat16)


def subtract(targets, matched, templates, coadd):
    images, tiles, band, _ = matched.shape
    steps = SUBTRACT_STEPS
    vmem = pl.BlockSpec(memory_space=pltpu.VMEM)
    return pl.pallas_call(
        functools.partial(subtract_kernel, tiles),
        grid=(steps,),
        in_specs=[pl.BlockSpec(memory_space=pltpu.SMEM), vmem, vmem, vmem],
        out_specs=[
            pl.BlockSpec((images // steps, band, tiles * TILE), lambda i: (i, 0, 0)),
            pl.BlockSpec(coadd.shape, lambda i: (0, 0)),
        ],
        out_shape=[
            jax.ShapeDtypeStruct((images, band, tiles * TILE), jnp.bfloat16),
            jax.ShapeDtypeStruct(coadd.shape, jnp.bfloat16),
        ],
        compiler_params=pltpu.CompilerParams(vmem_limit_bytes=32 << 20),
        name="subtract",
    )(targets, matched, templates, coadd)


def det_index(x, z, core, depth):
    return (x * depth + z) * 2 + core


class Links:
    def __init__(self, send_ref, recv_ref):
        self.send_ref, self.recv_ref = send_ref, recv_ref
        self.copies = {}

    def start(self, key, source, target, device):
        index = len(self.copies)
        copy = pltpu.make_async_remote_copy(
            src_ref=source,
            dst_ref=target,
            send_sem=self.send_ref.at[index],
            recv_sem=self.recv_ref.at[index],
            device_id=device,
            device_id_type=pl.DeviceIdType.MESH,
        )
        copy.start()
        self.copies[key] = copy

    def arrive(self, key):
        self.copies[key].wait_recv()

    def finish(self):
        for copy in self.copies.values():
            copy.wait_send()


def signed(place, step, way, size):
    return lax.rem(place + size + (step if way == 0 else -step), size)


def ring_reduce(links, tag, size, place, lead, rows, at, held_ref, whole_ref, half_ref, neighbour, base, finish):
    middle, half = size // 2, rows // 2

    def add(dest, extras, store):
        if base is not None:
            base(dest)

        def body(l, carry):
            for lo in (0, half):
                index = at(dest, l, lo, half)
                total = held_ref[index].astype(jnp.float32)
                if base is not None:
                    total = total + base.ref[base.index(dest, l, lo, half)].astype(jnp.float32)
                for ref, way, from_half in extras:
                    if not from_half:
                        total = total + ref[way, l, pl.ds(lo, half), :].astype(jnp.float32)
                    elif lo == way * half:
                        total = total + ref[way, l].astype(jnp.float32)
                store(l, lo, index, total)
            return carry

        lax.fori_loop(0, lead, body, 0)

    def put(l, lo, index, total):
        held_ref[index] = total.astype(jnp.bfloat16)

    far = signed(place, middle, 0, size)
    if base is not None:
        add(far, [], put)
    for way in (0, 1):
        links.start((tag, way, middle), held_ref.at[at(far, None, way * half, half)], half_ref.at[way], neighbour(way))
    yield
    for step in range(middle - 1, 0, -1):
        for way in (0, 1):
            dest = signed(place, step, way, size)
            links.arrive((tag, way, step + 1))
            source = (half_ref, way, True) if step + 1 == middle else (whole_ref.at[step], way, False)
            add(dest, [source], put)
            links.start(
                (tag, way, step), held_ref.at[at(dest, None, 0, rows)], whole_ref.at[step - 1, way], neighbour(way)
            )
        yield
    for way in (0, 1):
        links.arrive((tag, way, 1))
    add(place, [(whole_ref.at[0], 0, False), (whole_ref.at[0], 1, False)], put if finish is None else finish)
    yield


def ring_gather(links, tag, size, place, rows, view, neighbour, arrived):
    middle, half = size // 2, rows // 2
    for way in (0, 1):
        links.start((tag, way, 1), view(place, 0, rows), view(place, 0, rows), neighbour(way))
    arrived(place, 0)
    yield
    for step in range(1, middle):
        for way in (0, 1):
            origin = signed(place, step, 1 - way, size)
            links.arrive((tag, way, step))
            lo, length = (0, rows) if step + 1 < middle else (way * half, half)
            links.start((tag, way, step + 1), view(origin, lo, length), view(origin, lo, length), neighbour(way))
            arrived(origin, (step, way))
        yield
    for way in (0, 1):
        links.arrive((tag, way, middle))
    arrived(signed(place, middle, 0, size), middle)
    yield


def exchange_kernel(
    width,
    depth,
    split,
    total_ref,
    dense_ref,
    all_ref,
    coadd_ref,
    held_ref,
    az_ref,
    az_half,
    ax_ref,
    ax_half,
    bx_ref,
    bx_half,
    bz_ref,
    bz_half,
    send_ref,
    recv_ref,
):
    rows = dense_ref.shape[3]
    band = coadd_ref.shape[0]
    me = lax.axis_index("det")
    core = lax.rem(me, 2)
    z = lax.rem(me // 2, depth)
    x = me // (2 * depth)
    other = {"det": det_index(x, z, 1 - core, depth)}
    beside = [{"det": det_index(signed(x, 1, way, width), z, core, depth)} for way in (0, 1)]
    along = [{"det": det_index(x, signed(z, 1, way, depth), core, depth)} for way in (0, 1)]
    barrier = pltpu.get_barrier_semaphore()
    friends = [other] + beside + along
    for friend in friends:
        pl.semaphore_signal(barrier, inc=1, device_id=friend, device_id_type=pl.DeviceIdType.MESH)
    pl.semaphore_wait(barrier, len(friends))

    links = Links(send_ref, recv_ref)
    rest = rows - split

    def everything(l, size):
        return pl.ds(0, size) if l is None else l

    def a_at(dest, l, lo, length):
        return (everything(l, width), dest, pl.ds(lo, length), slice(None))

    def b_at(dest, l, lo, length):
        return (dest, everything(l, depth), pl.ds(split + lo, length), slice(None))

    def a_next(dest, l, lo, length):
        return (pl.ds(dest, 1) if l is None else dest, z, pl.ds(lo, length), slice(None))

    def b_next(dest, l, lo, length):
        return (pl.ds(x, 1) if l is None else x, dest, pl.ds(split + lo, length), slice(None))

    def with_core(index, which):
        return index[:2] + (which,) + index[2:]

    def hand_over(tag, dest, at, length):
        index = at(dest, None, 0, length)
        links.start(tag, dense_ref.at[with_core(index, 1 - core)], held_ref.at[index], other)

    zs = [(depth // 2, 0)] + [(s, w) for s in range(depth // 2 - 1, 0, -1) for w in (0, 1)] + [(0, 0)]
    xs = [(width // 2, 0)] + [(s, w) for s in range(width // 2 - 1, 0, -1) for w in (0, 1)] + [(0, 0)]
    turns = [("b", xs[0]), ("a", zs[0]), ("a", zs[1]), ("a", zs[2])]
    turns += [("b", k) for k in xs[1:-1]] + [("a", k) for k in zs[3:]] + [("b", xs[-1])]
    for part, (step, way) in turns:
        if part == "a":
            hand_over(("core a", step, way), signed(z, step, way, depth), a_at, split)
        else:
            hand_over(("core b", step, way), signed(x, step, way, width), b_at, rest)

    def base_of(tag, order, at):
        left = list(order)

        def base(dest):
            step, way = left.pop(0)
            links.arrive((tag, step, way))

        base.ref = dense_ref
        base.index = lambda *key: with_core(at(*key), core)
        return base

    def divided(offset):
        def store(l, lo, index, total):
            start, end = offset + lo, offset + lo + total.shape[0]
            while start < end:
                box = start // band
                stop = min(end, (box + 1) * band)
                part = total[start - offset - lo : stop - offset - lo] / total_ref[pl.ds(box, 1), :]
                part = part.astype(jnp.bfloat16)
                all_ref[x, z, core, pl.ds(start, stop - start), :] = part
                coadd_ref[pl.ds(start - box * band, stop - start), pl.ds(box * TILE, TILE)] = part
                start = stop

        return store

    a_first = ring_reduce(
        links, "a z", depth, z, width, split, a_at, held_ref, az_ref, az_half, lambda w: along[w],
        base_of("core a", zs, a_at), None,
    )
    b_first = ring_reduce(
        links, "b x", width, x, depth, rest, b_at, held_ref, bx_ref, bx_half, lambda w: beside[w],
        base_of("core b", xs, b_at), None,
    )
    a_second = ring_reduce(
        links, "a x", width, x, 1, split, a_next, held_ref, ax_ref, ax_half, lambda w: beside[w], None, divided(0)
    )
    b_second = ring_reduce(
        links, "b z", depth, z, 1, rest, b_next, held_ref, bz_ref, bz_half, lambda w: along[w], None, divided(split)
    )

    def a_view(origin, lo, length):
        return all_ref.at[:, origin, core, pl.ds(lo, length), :]

    def b_view(origin, lo, length):
        return all_ref.at[origin, :, core, pl.ds(split + lo, length), :]

    def a_own(origin, lo, length):
        return all_ref.at[origin, z, core, pl.ds(lo, length), :]

    def b_own(origin, lo, length):
        return all_ref.at[x, origin, core, pl.ds(split + lo, length), :]

    def nothing(origin, key):
        return None

    def across(tag, view, length):
        def arrived(origin, key):
            links.start((tag, key), view(origin, 0, length), view(origin, 0, length), other)

        return arrived

    a_third = ring_gather(links, "a gather x", width, x, split, a_own, lambda w: beside[w], nothing)
    b_third = ring_gather(links, "b gather z", depth, z, rest, b_own, lambda w: along[w], nothing)
    a_last = ring_gather(
        links, "a gather z", depth, z, split, a_view, lambda w: along[w], across("core a back", a_view, split)
    )
    b_last = ring_gather(
        links, "b gather x", width, x, rest, b_view, lambda w: beside[w], across("core b back", b_view, rest)
    )

    def chain(*parts):
        for part in parts:
            yield from part

    a_run = chain(a_first, a_second, a_third, a_last)
    b_run = chain(b_first, b_second, b_third, b_last)
    order = "ba" "a" "b" "aa" "ba" "baba" "bab" "bab" "abab" "b" "aabaabaab"
    runs = {"a": a_run, "b": b_run}
    for name in order:
        next(runs[name], None)
    for run in runs.values():
        for _ in run:
            pass
    for key in list(links.copies):
        if key[0] in ("core a back", "core b back"):
            links.arrive(key)
    links.finish()


def exchange(totals, dense, band, width, depth, split):
    rows = dense.shape[3]
    rest = rows - split
    copies = 2 * (2 * width + 2 * depth + 4) + 16

    def buffers(size, lead, length):
        return [
            pltpu.VMEM((size // 2 - 1, 2, lead, length, TILE), jnp.bfloat16),
            pltpu.VMEM((2, lead, length // 2, TILE), jnp.bfloat16),
        ]

    return pl.pallas_call(
        functools.partial(exchange_kernel, width, depth, split),
        in_specs=[pl.BlockSpec(memory_space=pltpu.VMEM)] * 2,
        out_specs=[pl.BlockSpec(memory_space=pltpu.VMEM)] * 2,
        out_shape=[
            jax.ShapeDtypeStruct(dense.shape, jnp.bfloat16),
            jax.ShapeDtypeStruct((band, rows // band * TILE), jnp.bfloat16),
        ],
        scratch_shapes=[pltpu.VMEM((width, depth, rows, TILE), jnp.bfloat16)]
        + buffers(depth, width, split)
        + buffers(width, 1, split)
        + buffers(width, depth, rest)
        + buffers(depth, 1, rest)
        + [pltpu.SemaphoreType.DMA((copies,)), pltpu.SemaphoreType.DMA((copies,))],
        compiler_params=pltpu.CompilerParams(
            collective_id=0, has_side_effects=True, vmem_limit_bytes=40 << 20
        ),
        name="exchange",
    )(totals, dense)


def gather_match_kernel(
    reach,
    offsets,
    coef_ref,
    taps_ref,
    patch_ref,
    block_ref,
    index_ref,
    levels_ref,
    home_ref,
    images_hbm,
    rows_hbm,
    cols_hbm,
    out_ref,
    total_ref,
    images_ref,
    rows_ref,
    cols_ref,
    full_ref,
    halo_ref,
    window_ref,
    left_ref,
    table_ref,
    load_ref,
    send_ref,
    recv_ref,
):
    count, band, side = images_hbm.shape
    half = band // 2
    size = full_ref.shape[1]
    me = lax.axis_index("row")
    beside = [signed(me, 1, way, size) for way in (0, 1)]

    def local(kind, image):
        source, target = ((images_hbm, images_ref), (cols_hbm, cols_ref), (rows_hbm, rows_ref))[kind]
        return pltpu.make_async_copy(source.at[image], target.at[image], load_ref.at[kind, image])

    def remote(kind, image, source, target, way):
        return pltpu.make_async_remote_copy(
            src_ref=source,
            dst_ref=target,
            send_sem=send_ref.at[kind, image],
            recv_sem=recv_ref.at[kind, image],
            device_id={"row": beside[way]},
            device_id_type=pl.DeviceIdType.MESH,
        )

    def own(image, way):
        place = full_ref.at[image, me]
        return remote(way, image, place, place, way)

    def forward(image, way):
        place = full_ref.at[image, beside[1 - way], pl.ds(way * half, half), :]
        return remote(2 + way, image, place, place, way)

    def edge(image, way):
        start = band - HALO if way == 0 else 0
        return remote(4 + way, image, rows_hbm.at[image, pl.ds(start, HALO), :], halo_ref.at[image, way], way)

    for kind in range(3):
        @pl.loop(0, count)
        def _(image):
            local(kind, image).start()

    barrier = pltpu.get_barrier_semaphore()
    for friend in beside:
        pl.semaphore_signal(barrier, inc=1, device_id={"row": friend}, device_id_type=pl.DeviceIdType.MESH)
    table_ref[...] = jnp.zeros_like(table_ref)
    keep = table_mask(2 * reach + 1)
    parts = tap_parts(taps_ref[...], offsets)
    visits = coef_ref.shape[1]
    first = jnp.where(me == 0, 0.0, 1.0)
    last = jnp.where(me == size - 1, 0.0, 1.0)
    pl.semaphore_wait(barrier, 2)

    @pl.loop(0, count + LAG)
    def _(step):
        @pl.when(step < count)
        def _():
            local(0, step).wait()
            local(1, step).wait()
            mapped = jnp.dot(images_ref[step], cols_ref[step], preferred_element_type=jnp.float32)
            full_ref[step, me] = mapped.astype(jnp.bfloat16)
            for way in (0, 1):
                own(step, way).start()
                edge(step, way).start()

        @pl.when(step == PASS_ON - 1)
        def _():
            denominators(patch_ref, block_ref, index_ref, levels_ref, home_ref, total_ref, out_ref.shape[1])

        @pl.when((step >= PASS_ON) & (step < count + PASS_ON))
        def _():
            image = step - PASS_ON
            for way in (0, 1):
                own(image, way).wait_recv()
                forward(image, way).start()

        @pl.when(step >= LAG)
        def _():
            image = step - LAG
            coef = coef_ref[image // visits, pl.ds(lax.rem(image, visits), 1), :]
            build_table(base_rows(coef, parts), keep, table_ref, offsets)
            local(2, image).wait()
            for way in (0, 1):
                forward(image, way).wait_recv()
                edge(image, way).wait_recv()
            rows = jnp.concatenate([halo_ref[image, 0], rows_ref[image], halo_ref[image, 1]], axis=0)
            full = full_ref[image].reshape(side, side)
            warped = jnp.dot(rows, full, preferred_element_type=jnp.float32)
            warped = jnp.concatenate(
                [warped[:HALO] * first, warped[HALO : HALO + band], warped[HALO + band :] * last], axis=0
            )
            convolve(warped, reach, window_ref, left_ref, table_ref, out_ref, image, offsets)

    @pl.loop(0, count)
    def _(image):
        for way in (0, 1):
            own(image, way).wait_send()
            forward(image, way).wait_send()
            edge(image, way).wait_send()


def gather_match(coef, taps, patch, block, index, levels, home, images, rows, cols, size):
    count, band, side = images.shape
    reach = (taps.shape[1] - 1) // 2
    offsets = 2 * reach + GROUP
    tiles = side // TILE
    hbm = pl.BlockSpec(memory_space=pltpu.MemorySpace.HBM)
    vmem = pl.BlockSpec(memory_space=pltpu.VMEM)
    smem = pl.BlockSpec(memory_space=pltpu.SMEM)
    return pl.pallas_call(
        functools.partial(gather_match_kernel, reach, offsets),
        in_specs=[vmem, vmem, vmem, vmem, vmem, smem, vmem, hbm, hbm, hbm],
        out_specs=[vmem, vmem],
        out_shape=[
            jax.ShapeDtypeStruct((count, tiles, band, TILE), jnp.float32),
            jax.ShapeDtypeStruct((8, TILE), jnp.float32),
        ],
        scratch_shapes=[
            pltpu.VMEM((count, band, side), jnp.bfloat16),
            pltpu.VMEM((count, band, side), jnp.bfloat16),
            pltpu.VMEM((count, side, side), jnp.bfloat16),
            pltpu.VMEM((count, size, band, side), jnp.bfloat16),
            pltpu.VMEM((count, 2, HALO, side), jnp.bfloat16),
            pltpu.VMEM((2 * tiles, band + 2 * HALO, TILE), jnp.float32),
            pltpu.VMEM((2 * tiles * (band // GROUP), offsets * TILE), jnp.bfloat16),
            pltpu.VMEM((offsets * TILE, 2 * TILE), jnp.bfloat16),
            pltpu.SemaphoreType.DMA((3, count)),
            pltpu.SemaphoreType.DMA((6, count)),
            pltpu.SemaphoreType.DMA((6, count)),
        ],
        compiler_params=pltpu.CompilerParams(
            collective_id=1, has_side_effects=True, vmem_limit_bytes=46 << 20
        ),
        name="gather_match",
    )(coef, taps, patch, block, index, levels, home, images, rows, cols)


def per_device(
    images,
    warp_rows,
    warp_cols,
    psf_coef,
    taps,
    dest_patch,
    dest_block,
    weight_index,
    weight_table,
    patch_home,
):
    dets, visits, band, cols = images.shape
    tiles = cols // TILE
    count = dets * visits
    patches = patch_home.shape[0]
    row_size = lax.axis_size("row")
    patch = dest_patch.reshape(-1, TILE)
    block = dest_block.reshape(-1, TILE)
    index = weight_index.T

    matched, totals = gather_match(
        psf_coef,
        taps,
        patch,
        block,
        index,
        weight_table,
        patch_home[None],
        images.reshape(count, band, cols),
        warp_rows.reshape(count, band, cols),
        warp_cols.reshape(count, cols, cols),
        row_size,
    )
    dense, targets = collect(patch, block, index, weight_table, patch_home, matched, patches * tiles)
    depth = DEPTH
    width = patches // (2 * depth)
    shape = (width, depth, 2, tiles * band, TILE)
    templates, coadd = exchange(totals, dense.reshape(shape), band, width, depth, SPLIT)
    difference, coadd = subtract(targets, matched, templates.reshape(patches * tiles, band, TILE), coadd)
    return (difference.reshape(dets, visits, band, cols), coadd[None])


def solution(mesh):
    placed = (
        P("det", None, "row", None),
        P("det", None, "row", None),
        P("det", None, None, None),
        P("det", None, None),
        P(),
        P(),
        P(),
        P(),
        P(),
        P(),
    )
    return jax.shard_map(
        per_device,
        mesh=mesh,
        in_specs=placed,
        out_specs=(P("det", None, "row", None), P("det", "row", None)),
        check_vma=False,
    )
```

```python
import functools

import jax
import jax.numpy as jnp
from jax import lax
from jax.experimental import pallas as pl
from jax.experimental.pallas import tpu as pltpu
from jax.sharding import PartitionSpec as P

TILE = 128
HALF = 64
HALO = 16
GROUP = 4
DEPTH = 8
STREAMS = (("a", "z", 0, 64), ("c", "z", 64, 64), ("b", "x", 128, 96), ("d", "x", 224, 64))
ORDER = "bcdacbaacdbbabddcaabdaccbdaacbbdabccddabacdbccdbbadcaddcbcadbacd"
PASS_ON = 2
LAG = 4
SUBTRACT_STEPS = 3


def one_hot(mask):
    return jnp.where(mask, 1.0, 0.0).astype(jnp.bfloat16)


def iota2(rows, cols, axis):
    return lax.broadcasted_iota(jnp.int32, (rows, cols), axis)


def tap_parts(taps, offsets):
    kernels, span = taps.shape
    shift = iota2(offsets, span, 0) - iota2(offsets, span, 1)

    def by_offset(late):
        pick = jnp.where(shift == late, 1.0, 0.0)
        return lax.dot_general(
            pick, taps, (((1,), (1,)), ((), ())), precision=lax.Precision.HIGHEST, preferred_element_type=jnp.float32
        )

    tap, lane = iota2(span, TILE, 0), iota2(span, TILE, 1)
    half = taps.astype(jnp.bfloat16)

    def placed(mask):
        return jnp.dot(half, one_hot(mask), preferred_element_type=jnp.float32).astype(jnp.bfloat16)

    here = placed((lane + tap == TILE) | ((tap == 0) & (lane == 0)))
    there = placed(lane + tap == HALF)
    return by_offset(0), by_offset(1), here, there


def base_rows(coef, parts):
    lead, late, here, there = parts
    left = jnp.dot((coef * lead).astype(jnp.bfloat16), here, preferred_element_type=jnp.float32)
    return left + jnp.dot((coef * late).astype(jnp.bfloat16), there, preferred_element_type=jnp.float32)


def denominators(patch_ref, block_ref, index_ref, table_ref, home_ref, out_ref, boxes):
    me = lax.axis_index("det")
    homes = home_ref[...]
    mine = jnp.sum(jnp.where(homes == me, iota2(1, homes.shape[1], 1), 0), axis=1, keepdims=True)
    visits, dets = index_ref.shape
    groups = dets // TILE
    period = visits * boxes
    row, lane = iota2(TILE, TILE, 0), iota2(TILE, TILE, 1)
    blank = jnp.zeros((8 - groups, TILE), jnp.float32)
    levels = []
    for visit in range(visits):
        parts = [index_ref[pl.ds(visit, 1), pl.ds(g * TILE, TILE)].astype(jnp.float32) for g in range(groups)]
        levels.append(jnp.concatenate(parts + [blank], axis=0).astype(jnp.bfloat16))
    sums = [jnp.zeros((groups, TILE), jnp.float32) for _ in range(boxes)]
    for k in range(period):
        level = jnp.zeros((8, TILE), jnp.float32)
        for visit in range(visits):
            gap = lane - period * row + (TILE * k - boxes * visit)
            level = level + jnp.dot(
                levels[visit], one_hot((gap >= 0) & (gap < boxes)), preferred_element_type=jnp.float32
            )
        level = level[:groups]
        weight = jnp.zeros((groups, TILE), jnp.float32)
        for n in range(table_ref.shape[0]):
            weight = jnp.where(level == float(n), table_ref[n], weight)
        patch = jnp.concatenate([patch_ref[pl.ds(g * period + k, 1), :] for g in range(groups)], axis=0)
        block = jnp.concatenate([block_ref[pl.ds(g * period + k, 1), :] for g in range(groups)], axis=0)
        for box in range(boxes):
            sums[box] = sums[box] + jnp.where((patch == mine) & (block == box), weight, 0.0)
    for box in range(boxes):
        total = jnp.sum(jnp.sum(sums[box], axis=0, keepdims=True), axis=1, keepdims=True)
        out_ref[pl.ds(box, 1), :] = jnp.broadcast_to(jnp.maximum(total, 1.0), (1, TILE))


def build_table(base, keep, table_ref, offsets):
    for t in range(offsets - 2):
        row = jnp.broadcast_to(base[t : t + 1], keep.shape)
        band = pltpu.roll(row, 0, 1, stride=1, stride_axis=0)
        band = jnp.where(keep, band, 0.0).astype(jnp.bfloat16)
        table_ref[pl.ds(t * TILE, keep.shape[0]), pl.ds(0, TILE)] = band
        table_ref[pl.ds((t + 2) * TILE, keep.shape[0]), pl.ds(TILE, TILE)] = band


def table_mask(span):
    rows = lax.broadcasted_iota(jnp.int32, (96, TILE), 0)
    lanes = lax.broadcasted_iota(jnp.int32, (96, TILE), 1)
    gap = rows - jnp.where(lanes >= HALF, lanes - HALF, lanes)
    return (gap >= 0) & (gap < span)


def convolve(warped, reach, window_ref, left_ref, table_ref, out_ref, image, offsets):
    rows, cols = warped.shape
    wide = jnp.concatenate([warped, jnp.zeros((rows, TILE), jnp.float32)], axis=1)
    even = pltpu.roll(wide, reach, 1)
    odd = pltpu.roll(wide, cols + TILE + reach - HALF, 1)
    tiles = cols // TILE
    groups = out_ref.shape[2] // GROUP
    for tile in range(tiles):
        window_ref[2 * tile] = even[:, tile * TILE : (tile + 1) * TILE]
        window_ref[2 * tile + 1] = odd[:, tile * TILE : (tile + 1) * TILE]
    for offset in range(offsets):
        start = HALO - reach + offset
        parts = [window_ref[w, pl.ds(start, groups, stride=GROUP), :] for w in range(2 * tiles)]
        left_ref[:, pl.ds(offset * TILE, TILE)] = jnp.concatenate(parts, axis=0).astype(jnp.bfloat16)
    product = jnp.dot(left_ref[...], table_ref[...], preferred_element_type=jnp.float32)
    low = lax.broadcasted_iota(jnp.int32, (groups, TILE), 1) < HALF
    for tile in range(tiles):
        for pair in range(2):
            first = product[(2 * tile) * groups : (2 * tile + 1) * groups, pair * TILE : (pair + 1) * TILE]
            second = product[(2 * tile + 1) * groups : (2 * tile + 2) * groups, pair * TILE : (pair + 1) * TILE]
            upper = jnp.where(low, first, pltpu.roll(second, HALF, 1))
            lower = jnp.where(low, pltpu.roll(first, HALF, 1), second)
            out_ref[image, tile, pl.ds(2 * pair, groups, stride=GROUP), :] = upper
            out_ref[image, tile, pl.ds(2 * pair + 1, groups, stride=GROUP), :] = lower


def collect_kernel(count, patch_ref, block_ref, index_ref, levels_ref, home_ref, matched_ref, dense_ref, target_ref):
    dets, tiles = count
    visits = index_ref.shape[0]
    me = lax.axis_index("det")
    dense_ref[...] = jnp.zeros_like(dense_ref)

    @pl.loop(0, dets)
    def _(det):
        for visit in range(visits):
            weight = levels_ref[index_ref[visit, me * dets + det]]
            for tile in range(tiles):
                local = (det * visits + visit) * tiles + tile
                piece = me * dets * visits * tiles + local
                row, lane = piece // TILE, lax.rem(piece, TILE)
                target = home_ref[patch_ref[row, lane]] * tiles + block_ref[row, lane]
                target_ref[local] = target
                value = (weight * matched_ref[det * visits + visit, tile]).astype(jnp.bfloat16)
                held = dense_ref[target].astype(jnp.float32)
                dense_ref[target] = (held + value.astype(jnp.float32)).astype(jnp.bfloat16)


def collect(patch, block, index, levels, home, matched, boxes):
    images, tiles, band, _ = matched.shape
    smem = pl.BlockSpec(memory_space=pltpu.SMEM)
    vmem = pl.BlockSpec(memory_space=pltpu.VMEM)
    return pl.pallas_call(
        functools.partial(collect_kernel, (images // index.shape[0], tiles)),
        in_specs=[smem] * 5 + [vmem],
        out_specs=[vmem, smem],
        out_shape=[
            jax.ShapeDtypeStruct((boxes, band, TILE), jnp.bfloat16),
            jax.ShapeDtypeStruct((images * tiles,), jnp.int32),
        ],
        compiler_params=pltpu.CompilerParams(vmem_limit_bytes=32 << 20),
        name="collect",
    )(patch, block, index, levels, home, matched)


def subtract_kernel(tiles, target_ref, matched_ref, template_ref, coadd_ref, out_ref, coadd_out):
    step = pl.program_id(0)
    images = out_ref.shape[0]

    @pl.when(step == 0)
    def _():
        coadd_out[...] = coadd_ref[...]

    @pl.loop(0, images)
    def _(local):
        image = step * images + local
        for tile in range(tiles):
            template = template_ref[target_ref[image * tiles + tile]].astype(jnp.float32)
            out_ref[local, :, pl.ds(tile * TILE, TILE)] = (matched_ref[image, tile] - template).astype(jnp.bfloat16)


def subtract(targets, matched, templates, coadd):
    images, tiles, band, _ = matched.shape
    steps = SUBTRACT_STEPS
    vmem = pl.BlockSpec(memory_space=pltpu.VMEM)
    return pl.pallas_call(
        functools.partial(subtract_kernel, tiles),
        grid=(steps,),
        in_specs=[pl.BlockSpec(memory_space=pltpu.SMEM), vmem, vmem, vmem],
        out_specs=[
            pl.BlockSpec((images // steps, band, tiles * TILE), lambda i: (i, 0, 0)),
            pl.BlockSpec(coadd.shape, lambda i: (0, 0)),
        ],
        out_shape=[
            jax.ShapeDtypeStruct((images, band, tiles * TILE), jnp.bfloat16),
            jax.ShapeDtypeStruct(coadd.shape, jnp.bfloat16),
        ],
        compiler_params=pltpu.CompilerParams(vmem_limit_bytes=32 << 20),
        name="subtract",
    )(targets, matched, templates, coadd)


def det_index(x, z, core, depth):
    return (x * depth + z) * 2 + core


class Links:
    def __init__(self, send_ref, recv_ref):
        self.send_ref, self.recv_ref = send_ref, recv_ref
        self.copies = {}

    def start(self, key, source, target, device):
        index = len(self.copies)
        copy = pltpu.make_async_remote_copy(
            src_ref=source,
            dst_ref=target,
            send_sem=self.send_ref.at[index],
            recv_sem=self.recv_ref.at[index],
            device_id=device,
            device_id_type=pl.DeviceIdType.MESH,
        )
        copy.start()
        self.copies[key] = copy

    def arrive(self, key):
        self.copies[key].wait_recv()

    def finish(self):
        for copy in self.copies.values():
            copy.wait_send()


def signed(place, step, way, size):
    return lax.rem(place + size + (step if way == 0 else -step), size)


def ring_reduce(links, tag, size, place, lead, rows, at, held_ref, whole_ref, half_ref, neighbour, base, finish):
    middle, half = size // 2, rows // 2

    def add(dest, extras, store):
        if base is not None:
            base(dest)

        def body(l, carry):
            for lo in (0, half):
                index = at(dest, l, lo, half)
                total = held_ref[index].astype(jnp.float32)
                if base is not None:
                    total = total + base.ref[base.index(dest, l, lo, half)].astype(jnp.float32)
                for ref, way, from_half in extras:
                    if not from_half:
                        total = total + ref[way, l, pl.ds(lo, half), :].astype(jnp.float32)
                    elif lo == way * half:
                        total = total + ref[way, l].astype(jnp.float32)
                store(l, lo, index, total)
            return carry

        lax.fori_loop(0, lead, body, 0)

    def put(l, lo, index, total):
        held_ref[index] = total.astype(jnp.bfloat16)

    far = signed(place, middle, 0, size)
    if base is not None:
        add(far, [], put)
    for way in (0, 1):
        links.start((tag, way, middle), held_ref.at[at(far, None, way * half, half)], half_ref.at[way], neighbour(way))
    yield
    for step in range(middle - 1, 0, -1):
        for way in (0, 1):
            dest = signed(place, step, way, size)
            links.arrive((tag, way, step + 1))
            source = (half_ref, way, True) if step + 1 == middle else (whole_ref.at[step], way, False)
            add(dest, [source], put)
            links.start(
                (tag, way, step), held_ref.at[at(dest, None, 0, rows)], whole_ref.at[step - 1, way], neighbour(way)
            )
        yield
    for way in (0, 1):
        links.arrive((tag, way, 1))
    add(place, [(whole_ref.at[0], 0, False), (whole_ref.at[0], 1, False)], put if finish is None else finish)
    yield


def ring_gather(links, tag, size, place, rows, view, neighbour, arrived):
    middle, half = size // 2, rows // 2
    for way in (0, 1):
        links.start((tag, way, 1), view(place, 0, rows), view(place, 0, rows), neighbour(way))
    arrived(place, 0)
    yield
    for step in range(1, middle):
        for way in (0, 1):
            origin = signed(place, step, 1 - way, size)
            links.arrive((tag, way, step))
            lo, length = (0, rows) if step + 1 < middle else (way * half, half)
            links.start((tag, way, step + 1), view(origin, lo, length), view(origin, lo, length), neighbour(way))
            arrived(origin, (step, way))
        yield
    for way in (0, 1):
        links.arrive((tag, way, middle))
    arrived(signed(place, middle, 0, size), middle)
    yield


def chunk_order(size):
    middle = size // 2
    return [[(middle, 0)]] + [[(step, 0), (step, 1)] for step in range(middle - 1, 0, -1)] + [[(0, 0)]]


def exchange_kernel(width, depth, total_ref, dense_ref, all_ref, coadd_ref, held_ref, send_ref, recv_ref, *buffers):
    band = coadd_ref.shape[0]
    me = lax.axis_index("det")
    core = lax.rem(me, 2)
    z = lax.rem(me // 2, depth)
    x = me // (2 * depth)
    other = {"det": det_index(x, z, 1 - core, depth)}
    ways = {
        "x": [{"det": det_index(signed(x, 1, way, width), z, core, depth)} for way in (0, 1)],
        "z": [{"det": det_index(x, signed(z, 1, way, depth), core, depth)} for way in (0, 1)],
    }
    sizes, places = {"x": width, "z": depth}, {"x": x, "z": z}
    barrier = pltpu.get_barrier_semaphore()
    friends = [other] + ways["x"] + ways["z"]
    for friend in friends:
        pl.semaphore_signal(barrier, inc=1, device_id=friend, device_id_type=pl.DeviceIdType.MESH)
    pl.semaphore_wait(barrier, len(friends))
    links = Links(send_ref, recv_ref)

    def with_core(index, which):
        return index[:2] + (which,) + index[2:]

    def indices(first, start):
        second = "x" if first == "z" else "z"

        def order(dest, across):
            return (across, dest) if first == "z" else (dest, across)

        def wide(dest, l, lo, length):
            across = pl.ds(0, sizes[second]) if l is None else l
            return order(dest, across) + (pl.ds(start + lo, length), slice(None))

        def narrow(dest, l, lo, length):
            across = pl.ds(places[first], 1) if l is None else places[first]
            return order(across, dest) + (pl.ds(start + lo, length), slice(None))

        return second, wide, narrow

    def stream(name, first, start, rows, refs):
        second, wide, narrow = indices(first, start)
        left = [c for step in chunk_order(sizes[first]) for c in step]

        def base(dest):
            links.arrive((name, "core") + left.pop(0))

        base.ref = dense_ref
        base.index = lambda *key: with_core(wide(*key), core)

        def store(l, lo, index, total):
            begin, end = start + lo, start + lo + total.shape[0]
            while begin < end:
                box = begin // band
                stop = min(end, (box + 1) * band)
                part = total[begin - start - lo : stop - start - lo] / total_ref[pl.ds(box, 1), :]
                part = part.astype(jnp.bfloat16)
                all_ref[x, z, core, pl.ds(begin, stop - begin), :] = part
                coadd_ref[pl.ds(begin - box * band, stop - begin), pl.ds(box * TILE, TILE)] = part
                begin = stop

        def view(maker):
            return lambda origin, lo, length: all_ref.at[with_core(maker(origin, None, lo, length), core)]

        def nothing(origin, key):
            return None

        def across(origin, key):
            place = view(wide)(origin, 0, rows)
            links.start((name, "back", key), place, place, other)

        yield from ring_reduce(
            links, (name, 1), sizes[first], places[first], sizes[second], rows, wide, held_ref,
            refs[0], refs[1], lambda w: ways[first][w], base, None,
        )
        yield from ring_reduce(
            links, (name, 2), sizes[second], places[second], 1, rows, narrow, held_ref,
            refs[2], refs[3], lambda w: ways[second][w], None, store,
        )
        yield from ring_gather(
            links, (name, 3), sizes[second], places[second], rows, view(narrow), lambda w: ways[second][w], nothing
        )
        yield from ring_gather(
            links, (name, 4), sizes[first], places[first], rows, view(wide), lambda w: ways[first][w], across
        )

    firsts = {name: (first, start, rows) for name, first, start, rows in STREAMS}
    waiting = {name: chunk_order(sizes[firsts[name][0]]) for name in firsts}
    for name in ORDER:
        if not waiting[name]:
            continue
        first, start, rows = firsts[name]
        wide = indices(first, start)[1]
        for step, way in waiting[name].pop(0):
            index = wide(signed(places[first], step, way, sizes[first]), None, 0, rows)
            links.start((name, "core", step, way), dense_ref.at[with_core(index, 1 - core)], held_ref.at[index], other)

    runs = {}
    for number, (name, first, start, rows) in enumerate(STREAMS):
        runs[name] = stream(name, first, start, rows, buffers[4 * number : 4 * number + 4])
    for name in ORDER:
        next(runs[name], None)
    for run in runs.values():
        for _ in run:
            pass
    for key in list(links.copies):
        if key[1] == "back":
            links.arrive(key)
    links.finish()


def exchange(totals, dense, band, width, depth):
    rows = dense.shape[3]
    sizes = {"x": width, "z": depth}
    copies = 0
    scratch = []
    for name, first, start, length in STREAMS:
        size, other = sizes[first], width + depth - sizes[first]
        copies += 4 * (size + other) + 2 * size
        for places, lead in ((size, other), (other, 1)):
            scratch.append(pltpu.VMEM((places // 2 - 1, 2, lead, length, TILE), jnp.bfloat16))
            scratch.append(pltpu.VMEM((2, lead, length // 2, TILE), jnp.bfloat16))
    return pl.pallas_call(
        functools.partial(exchange_kernel, width, depth),
        in_specs=[pl.BlockSpec(memory_space=pltpu.VMEM)] * 2,
        out_specs=[pl.BlockSpec(memory_space=pltpu.VMEM)] * 2,
        out_shape=[
            jax.ShapeDtypeStruct(dense.shape, jnp.bfloat16),
            jax.ShapeDtypeStruct((band, rows // band * TILE), jnp.bfloat16),
        ],
        scratch_shapes=[
            pltpu.VMEM((width, depth, rows, TILE), jnp.bfloat16),
            pltpu.SemaphoreType.DMA((copies,)),
            pltpu.SemaphoreType.DMA((copies,)),
        ]
        + scratch,
        compiler_params=pltpu.CompilerParams(
            collective_id=0, has_side_effects=True, vmem_limit_bytes=40 << 20
        ),
        name="exchange",
    )(totals, dense)


def gather_match_kernel(
    reach,
    offsets,
    coef_ref,
    taps_ref,
    patch_ref,
    block_ref,
    index_ref,
    levels_ref,
    home_ref,
    images_hbm,
    rows_hbm,
    cols_hbm,
    out_hbm,
    total_ref,
    out_ref,
    images_ref,
    rows_ref,
    cols_ref,
    full_ref,
    halo_ref,
    window_ref,
    left_ref,
    table_ref,
    load_ref,
    save_ref,
    send_ref,
    recv_ref,
):
    count, band, side = images_hbm.shape
    half = band // 2
    size = full_ref.shape[1]
    me = lax.axis_index("row")
    beside = [signed(me, 1, way, size) for way in (0, 1)]

    def local(kind, image):
        source, target = ((images_hbm, images_ref), (cols_hbm, cols_ref), (rows_hbm, rows_ref))[kind]
        return pltpu.make_async_copy(source.at[image], target.at[image], load_ref.at[kind, image])

    def remote(kind, image, source, target, way):
        return pltpu.make_async_remote_copy(
            src_ref=source,
            dst_ref=target,
            send_sem=send_ref.at[kind, image],
            recv_sem=recv_ref.at[kind, image],
            device_id={"row": beside[way]},
            device_id_type=pl.DeviceIdType.MESH,
        )

    def own(image, way):
        place = full_ref.at[image, me]
        return remote(way, image, place, place, way)

    def forward(image, way):
        place = full_ref.at[image, beside[1 - way], pl.ds(way * half, half), :]
        return remote(2 + way, image, place, place, way)

    def edge(image, way):
        start = band - HALO if way == 0 else 0
        return remote(4 + way, image, rows_hbm.at[image, pl.ds(start, HALO), :], halo_ref.at[image, way], way)

    def save(image):
        slot = lax.rem(image, 2)
        return pltpu.make_async_copy(out_ref.at[slot], out_hbm.at[image], save_ref.at[slot])

    for kind in range(3):
        @pl.loop(0, count)
        def _(image):
            local(kind, image).start()

    barrier = pltpu.get_barrier_semaphore()
    for friend in beside:
        pl.semaphore_signal(barrier, inc=1, device_id={"row": friend}, device_id_type=pl.DeviceIdType.MESH)
    table_ref[...] = jnp.zeros_like(table_ref)
    keep = table_mask(2 * reach + 1)
    parts = tap_parts(taps_ref[...], offsets)
    visits = coef_ref.shape[1]
    first = jnp.where(me == 0, 0.0, 1.0)
    last = jnp.where(me == size - 1, 0.0, 1.0)
    pl.semaphore_wait(barrier, 2)

    @pl.loop(0, count + LAG)
    def _(step):
        @pl.when(step < count)
        def _():
            local(0, step).wait()
            local(1, step).wait()
            mapped = jnp.dot(images_ref[step], cols_ref[step], preferred_element_type=jnp.float32)
            full_ref[step, me] = mapped.astype(jnp.bfloat16)
            for way in (0, 1):
                own(step, way).start()
                edge(step, way).start()

        @pl.when(step == PASS_ON - 1)
        def _():
            denominators(patch_ref, block_ref, index_ref, levels_ref, home_ref, total_ref, out_ref.shape[1])

        @pl.when((step >= PASS_ON) & (step < count + PASS_ON))
        def _():
            image = step - PASS_ON
            for way in (0, 1):
                own(image, way).wait_recv()
                forward(image, way).start()

        @pl.when(step >= LAG)
        def _():
            image = step - LAG
            coef = coef_ref[image // visits, pl.ds(lax.rem(image, visits), 1), :]
            build_table(base_rows(coef, parts), keep, table_ref, offsets)
            local(2, image).wait()
            for way in (0, 1):
                forward(image, way).wait_recv()
                edge(image, way).wait_recv()
            rows = jnp.concatenate([halo_ref[image, 0], rows_ref[image], halo_ref[image, 1]], axis=0)
            full = full_ref[image].reshape(side, side)
            warped = jnp.dot(rows, full, preferred_element_type=jnp.float32)
            warped = jnp.concatenate(
                [warped[:HALO] * first, warped[HALO : HALO + band], warped[HALO + band :] * last], axis=0
            )
            @pl.when(image >= 2)
            def _():
                save(image - 2).wait()

            convolve(warped, reach, window_ref, left_ref, table_ref, out_ref, lax.rem(image, 2), offsets)
            save(image).start()

    for image in (count - 2, count - 1):
        save(image).wait()

    @pl.loop(0, count)
    def _(image):
        for way in (0, 1):
            own(image, way).wait_send()
            forward(image, way).wait_send()
            edge(image, way).wait_send()


def gather_match(coef, taps, patch, block, index, levels, home, images, rows, cols, size):
    count, band, side = images.shape
    reach = (taps.shape[1] - 1) // 2
    offsets = 2 * reach + GROUP
    tiles = side // TILE
    hbm = pl.BlockSpec(memory_space=pltpu.MemorySpace.HBM)
    vmem = pl.BlockSpec(memory_space=pltpu.VMEM)
    smem = pl.BlockSpec(memory_space=pltpu.SMEM)
    return pl.pallas_call(
        functools.partial(gather_match_kernel, reach, offsets),
        in_specs=[vmem, vmem, vmem, vmem, vmem, smem, vmem, hbm, hbm, hbm],
        out_specs=[hbm, vmem],
        out_shape=[
            jax.ShapeDtypeStruct((count, tiles, band, TILE), jnp.float32),
            jax.ShapeDtypeStruct((8, TILE), jnp.float32),
        ],
        scratch_shapes=[
            pltpu.VMEM((2, tiles, band, TILE), jnp.float32),
            pltpu.VMEM((count, band, side), jnp.bfloat16),
            pltpu.VMEM((count, band, side), jnp.bfloat16),
            pltpu.VMEM((count, side, side), jnp.bfloat16),
            pltpu.VMEM((count, size, band, side), jnp.bfloat16),
            pltpu.VMEM((count, 2, HALO, side), jnp.bfloat16),
            pltpu.VMEM((2 * tiles, band + 2 * HALO, TILE), jnp.float32),
            pltpu.VMEM((2 * tiles * (band // GROUP), offsets * TILE), jnp.bfloat16),
            pltpu.VMEM((offsets * TILE, 2 * TILE), jnp.bfloat16),
            pltpu.SemaphoreType.DMA((3, count)),
            pltpu.SemaphoreType.DMA((2,)),
            pltpu.SemaphoreType.DMA((6, count)),
            pltpu.SemaphoreType.DMA((6, count)),
        ],
        compiler_params=pltpu.CompilerParams(
            collective_id=1, has_side_effects=True, vmem_limit_bytes=58 << 20
        ),
        name="gather_match",
    )(coef, taps, patch, block, index, levels, home, images, rows, cols)


def per_device(
    images,
    warp_rows,
    warp_cols,
    psf_coef,
    taps,
    dest_patch,
    dest_block,
    weight_index,
    weight_table,
    patch_home,
):
    dets, visits, band, cols = images.shape
    tiles = cols // TILE
    count = dets * visits
    patches = patch_home.shape[0]
    row_size = lax.axis_size("row")
    patch = dest_patch.reshape(-1, TILE)
    block = dest_block.reshape(-1, TILE)
    index = weight_index.T

    matched, totals = gather_match(
        psf_coef,
        taps,
        patch,
        block,
        index,
        weight_table,
        patch_home[None],
        images.reshape(count, band, cols),
        warp_rows.reshape(count, band, cols),
        warp_cols.reshape(count, cols, cols),
        row_size,
    )
    dense, targets = collect(patch, block, index, weight_table, patch_home, matched, patches * tiles)
    depth = DEPTH
    width = patches // (2 * depth)
    shape = (width, depth, 2, tiles * band, TILE)
    templates, coadd = exchange(totals, dense.reshape(shape), band, width, depth)
    difference, coadd = subtract(targets, matched, templates.reshape(patches * tiles, band, TILE), coadd)
    return (difference.reshape(dets, visits, band, cols), coadd[None])


def solution(mesh):
    placed = (
        P("det", None, "row", None),
        P("det", None, "row", None),
        P("det", None, None, None),
        P("det", None, None),
        P(),
        P(),
        P(),
        P(),
        P(),
        P(),
    )
    return jax.shard_map(
        per_device,
        mesh=mesh,
        in_specs=placed,
        out_specs=(P("det", None, "row", None), P("det", "row", None)),
        check_vma=False,
    )
```

```python
import functools

import jax
import jax.numpy as jnp
from jax import lax
from jax.experimental import pallas as pl
from jax.experimental.pallas import tpu as pltpu
from jax.sharding import PartitionSpec as P

TILE = 128
HALF = 64
HALO = 16
GROUP = 4
DEPTH = 8
STREAMS = (("a", "z", 0, 32), ("c", "z", 32, 64), ("b", "x", 96, 64), ("d", "x", 160, 64), ("e", "x", 224, 64))
ORDER = "bcedbadecbadbecadcbeadcbeacdabecdaecdbaecbdea"
PASS_ON = 2
LAG = 4
SUBTRACT_STEPS = 3


def one_hot(mask):
    return jnp.where(mask, 1.0, 0.0).astype(jnp.bfloat16)


def iota2(rows, cols, axis):
    return lax.broadcasted_iota(jnp.int32, (rows, cols), axis)


def tap_parts(taps, offsets):
    kernels, span = taps.shape
    shift = iota2(offsets, span, 0) - iota2(offsets, span, 1)

    def by_offset(late):
        pick = jnp.where(shift == late, 1.0, 0.0)
        return lax.dot_general(
            pick, taps, (((1,), (1,)), ((), ())), precision=lax.Precision.HIGHEST, preferred_element_type=jnp.float32
        )

    tap, lane = iota2(span, TILE, 0), iota2(span, TILE, 1)
    half = taps.astype(jnp.bfloat16)

    def placed(mask):
        return jnp.dot(half, one_hot(mask), preferred_element_type=jnp.float32).astype(jnp.bfloat16)

    here = placed((lane + tap == TILE) | ((tap == 0) & (lane == 0)))
    there = placed(lane + tap == HALF)
    return by_offset(0), by_offset(1), here, there


def base_rows(coef, parts):
    lead, late, here, there = parts
    left = jnp.dot((coef * lead).astype(jnp.bfloat16), here, preferred_element_type=jnp.float32)
    return left + jnp.dot((coef * late).astype(jnp.bfloat16), there, preferred_element_type=jnp.float32)


def denominators(patch_ref, block_ref, index_ref, table_ref, home_ref, out_ref, boxes):
    me = lax.axis_index("det")
    homes = home_ref[...]
    mine = jnp.sum(jnp.where(homes == me, iota2(1, homes.shape[1], 1), 0), axis=1, keepdims=True)
    visits, dets = index_ref.shape
    groups = dets // TILE
    period = visits * boxes
    row, lane = iota2(TILE, TILE, 0), iota2(TILE, TILE, 1)
    blank = jnp.zeros((8 - groups, TILE), jnp.float32)
    levels = []
    for visit in range(visits):
        parts = [index_ref[pl.ds(visit, 1), pl.ds(g * TILE, TILE)].astype(jnp.float32) for g in range(groups)]
        levels.append(jnp.concatenate(parts + [blank], axis=0).astype(jnp.bfloat16))
    sums = [jnp.zeros((groups, TILE), jnp.float32) for _ in range(boxes)]
    for k in range(period):
        level = jnp.zeros((8, TILE), jnp.float32)
        for visit in range(visits):
            gap = lane - period * row + (TILE * k - boxes * visit)
            level = level + jnp.dot(
                levels[visit], one_hot((gap >= 0) & (gap < boxes)), preferred_element_type=jnp.float32
            )
        level = level[:groups]
        weight = jnp.zeros((groups, TILE), jnp.float32)
        for n in range(table_ref.shape[0]):
            weight = jnp.where(level == float(n), table_ref[n], weight)
        patch = jnp.concatenate(
            [patch_ref[:, pl.ds((g * period + k) * TILE, TILE)] for g in range(groups)], axis=0
        )
        block = jnp.concatenate([block_ref[pl.ds(g * period + k, 1), :] for g in range(groups)], axis=0)
        for box in range(boxes):
            sums[box] = sums[box] + jnp.where((patch == mine) & (block == box), weight, 0.0)
    for box in range(boxes):
        total = jnp.sum(jnp.sum(sums[box], axis=0, keepdims=True), axis=1, keepdims=True)
        out_ref[pl.ds(box, 1), :] = jnp.broadcast_to(jnp.maximum(total, 1.0), (1, TILE))


def build_table(base, keep, table_ref, offsets):
    for t in range(offsets - 2):
        row = jnp.broadcast_to(base[t : t + 1], keep.shape)
        band = pltpu.roll(row, 0, 1, stride=1, stride_axis=0)
        band = jnp.where(keep, band, 0.0).astype(jnp.bfloat16)
        table_ref[pl.ds(t * TILE, keep.shape[0]), pl.ds(0, TILE)] = band
        table_ref[pl.ds((t + 2) * TILE, keep.shape[0]), pl.ds(TILE, TILE)] = band


def table_mask(span):
    rows = lax.broadcasted_iota(jnp.int32, (96, TILE), 0)
    lanes = lax.broadcasted_iota(jnp.int32, (96, TILE), 1)
    gap = rows - jnp.where(lanes >= HALF, lanes - HALF, lanes)
    return (gap >= 0) & (gap < span)


def convolve(warped, reach, window_ref, left_ref, table_ref, out_ref, image, offsets):
    rows, cols = warped.shape
    wide = jnp.concatenate([warped, jnp.zeros((rows, TILE), jnp.float32)], axis=1)
    even = pltpu.roll(wide, reach, 1)
    odd = pltpu.roll(wide, cols + TILE + reach - HALF, 1)
    tiles = cols // TILE
    groups = out_ref.shape[2] // GROUP
    for tile in range(tiles):
        window_ref[2 * tile] = even[:, tile * TILE : (tile + 1) * TILE]
        window_ref[2 * tile + 1] = odd[:, tile * TILE : (tile + 1) * TILE]
    for offset in range(offsets):
        start = HALO - reach + offset
        parts = [window_ref[w, pl.ds(start, groups, stride=GROUP), :] for w in range(2 * tiles)]
        left_ref[:, pl.ds(offset * TILE, TILE)] = jnp.concatenate(parts, axis=0).astype(jnp.bfloat16)
    product = jnp.dot(left_ref[...], table_ref[...], preferred_element_type=jnp.float32)
    low = lax.broadcasted_iota(jnp.int32, (groups, TILE), 1) < HALF
    for tile in range(tiles):
        for pair in range(2):
            first = product[(2 * tile) * groups : (2 * tile + 1) * groups, pair * TILE : (pair + 1) * TILE]
            second = product[(2 * tile + 1) * groups : (2 * tile + 2) * groups, pair * TILE : (pair + 1) * TILE]
            upper = jnp.where(low, first, pltpu.roll(second, HALF, 1))
            lower = jnp.where(low, pltpu.roll(first, HALF, 1), second)
            out_ref[image, tile, pl.ds(2 * pair, groups, stride=GROUP), :] = upper
            out_ref[image, tile, pl.ds(2 * pair + 1, groups, stride=GROUP), :] = lower


def collect_kernel(count, patch_ref, block_ref, index_ref, levels_ref, home_ref, matched_ref, dense_ref, target_ref):
    dets, tiles = count
    visits = index_ref.shape[0]
    me = lax.axis_index("det")
    dense_ref[...] = jnp.zeros_like(dense_ref)

    @pl.loop(0, dets)
    def _(det):
        for visit in range(visits):
            weight = levels_ref[index_ref[visit, me * dets + det]]
            for tile in range(tiles):
                local = (det * visits + visit) * tiles + tile
                piece = me * dets * visits * tiles + local
                row, lane = piece // TILE, lax.rem(piece, TILE)
                target = home_ref[patch_ref[0, piece]] * tiles + block_ref[row, lane]
                target_ref[local] = target
                value = (weight * matched_ref[det * visits + visit, tile]).astype(jnp.bfloat16)
                held = dense_ref[target].astype(jnp.float32)
                dense_ref[target] = (held + value.astype(jnp.float32)).astype(jnp.bfloat16)


def collect(patch, block, index, levels, home, matched, boxes):
    images, tiles, band, _ = matched.shape
    smem = pl.BlockSpec(memory_space=pltpu.SMEM)
    vmem = pl.BlockSpec(memory_space=pltpu.VMEM)
    return pl.pallas_call(
        functools.partial(collect_kernel, (images // index.shape[0], tiles)),
        in_specs=[smem] * 5 + [vmem],
        out_specs=[vmem, smem],
        out_shape=[
            jax.ShapeDtypeStruct((boxes, band, TILE), jnp.bfloat16),
            jax.ShapeDtypeStruct((images * tiles,), jnp.int32),
        ],
        compiler_params=pltpu.CompilerParams(vmem_limit_bytes=32 << 20),
        name="collect",
    )(patch, block, index, levels, home, matched)


def subtract_kernel(tiles, target_ref, matched_ref, template_ref, coadd_ref, out_ref, coadd_out):
    step = pl.program_id(0)
    images = out_ref.shape[0]

    @pl.when(step == 0)
    def _():
        coadd_out[...] = coadd_ref[...]

    @pl.loop(0, images)
    def _(local):
        image = step * images + local
        for tile in range(tiles):
            template = template_ref[target_ref[image * tiles + tile]].astype(jnp.float32)
            out_ref[local, :, pl.ds(tile * TILE, TILE)] = (matched_ref[image, tile] - template).astype(jnp.bfloat16)


def subtract(targets, matched, templates, coadd):
    images, tiles, band, _ = matched.shape
    steps = SUBTRACT_STEPS
    vmem = pl.BlockSpec(memory_space=pltpu.VMEM)
    return pl.pallas_call(
        functools.partial(subtract_kernel, tiles),
        grid=(steps,),
        in_specs=[pl.BlockSpec(memory_space=pltpu.SMEM), vmem, vmem, vmem],
        out_specs=[
            pl.BlockSpec((images // steps, band, tiles * TILE), lambda i: (i, 0, 0)),
            pl.BlockSpec(coadd.shape, lambda i: (0, 0)),
        ],
        out_shape=[
            jax.ShapeDtypeStruct((images, band, tiles * TILE), jnp.bfloat16),
            jax.ShapeDtypeStruct(coadd.shape, jnp.bfloat16),
        ],
        compiler_params=pltpu.CompilerParams(vmem_limit_bytes=32 << 20),
        name="subtract",
    )(targets, matched, templates, coadd)


def det_index(x, z, core, depth):
    return (x * depth + z) * 2 + core


class Links:
    def __init__(self, send_ref, recv_ref):
        self.send_ref, self.recv_ref = send_ref, recv_ref
        self.copies = {}

    def start(self, key, source, target, device):
        index = len(self.copies)
        copy = pltpu.make_async_remote_copy(
            src_ref=source,
            dst_ref=target,
            send_sem=self.send_ref.at[index],
            recv_sem=self.recv_ref.at[index],
            device_id=device,
            device_id_type=pl.DeviceIdType.MESH,
        )
        copy.start()
        self.copies[key] = copy

    def arrive(self, key):
        self.copies[key].wait_recv()

    def finish(self):
        for copy in self.copies.values():
            copy.wait_send()


def signed(place, step, way, size):
    return lax.rem(place + size + (step if way == 0 else -step), size)


def adder(dest_at, lead, half, held_ref, base):
    def add(dest, extras, store):
        if base is not None:
            base(dest)

        def body(l, carry):
            for lo in (0, half):
                index = dest_at(dest, l, lo, half)
                total = held_ref[index].astype(jnp.float32)
                if base is not None:
                    total = total + base.ref[base.index(dest, l, lo, half)].astype(jnp.float32)
                for ref, way, from_half in extras:
                    if not from_half:
                        total = total + ref[way, l, pl.ds(lo, half), :].astype(jnp.float32)
                    elif lo == way * half:
                        total = total + ref[way, l].astype(jnp.float32)
                store(l, lo, index, total)
            return carry

        lax.fori_loop(0, lead, body, 0)

    return add


def ring_reduce(links, tag, size, place, lead, rows, at, held_ref, whole_ref, half_ref, device, base, finish):
    middle, half = size // 2, rows // 2
    add = adder(at, lead, half, held_ref, base)

    def put(l, lo, index, total):
        held_ref[index] = total.astype(jnp.bfloat16)

    def send(key, dest, buffer, way, distance, lo=0, length=rows):
        links.start((tag, way, key), held_ref.at[at(dest, None, lo, length)], buffer, device(way, distance))

    relay = middle // 2
    far = signed(place, middle, 0, size)
    if base is not None:
        add(far, [], put)
    for way in (0, 1):
        send(middle, far, half_ref.at[way], way, relay, way * half, half)
    for step in range(middle - 1, 0, -1):
        if step == relay:
            continue
        for way in (0, 1):
            dest = signed(place, step, way, size)
            if base is not None:
                add(dest, [], put)
            send(step, dest, whole_ref.at[step - 1, way], way, step - relay if step > relay else step)
    yield
    for way in (0, 1):
        dest = signed(place, relay, way, size)
        sources = [(half_ref, way, True)]
        links.arrive((tag, way, middle))
        for step in range(relay + 1, middle):
            links.arrive((tag, way, step))
            sources.append((whole_ref.at[step - 1], way, False))
        add(dest, sources, put)
        send(relay, dest, whole_ref.at[relay - 1, way], way, relay)
    yield
    last = [(step, way) for step in range(1, relay + 1) for way in (0, 1)]
    for step, way in last:
        links.arrive((tag, way, step))
    add(place, [(whole_ref.at[step - 1], way, False) for step, way in last], put if finish is None else finish)


def ring_gather(links, tag, size, place, rows, view, device, arrived):
    middle, half = size // 2, rows // 2
    relay = middle // 2

    def send(key, origin, way, distance, lo=0, length=rows):
        part = view(origin, lo, length)
        links.start((tag, way, key), part, part, device(way, distance))

    for step in range(relay, 0, -1):
        for way in (0, 1):
            send(step, place, way, step)
    arrived(place, 0)
    yield
    for way in (0, 1):
        origin = signed(place, relay, 1 - way, size)
        links.arrive((tag, way, relay))
        for step in range(relay + 1, middle):
            send(step, origin, way, step - relay)
        send(middle, origin, way, relay, way * half, half)
        arrived(origin, (relay, way))
    for step in range(1, middle):
        if step < relay:
            for way in (0, 1):
                links.arrive((tag, way, step))
                arrived(signed(place, step, 1 - way, size), (step, way))
    yield
    for step in range(relay + 1, middle):
        for way in (0, 1):
            links.arrive((tag, way, step))
            arrived(signed(place, step, 1 - way, size), (step, way))
    for way in (0, 1):
        links.arrive((tag, way, middle))
    arrived(signed(place, middle, 0, size), middle)


def chunk_order(size):
    middle = size // 2
    relay = middle // 2
    first = [(middle, 0)] + [(step, way) for step in range(middle - 1, 0, -1) if step != relay for way in (0, 1)]
    return [first, [(relay, 0), (relay, 1)], [(0, 0)]]


def exchange_kernel(width, depth, total_ref, dense_ref, all_ref, coadd_ref, held_ref, send_ref, recv_ref, *buffers):
    band = coadd_ref.shape[0]
    me = lax.axis_index("det")
    core = lax.rem(me, 2)
    z = lax.rem(me // 2, depth)
    x = me // (2 * depth)
    other = {"det": det_index(x, z, 1 - core, depth)}

    def device(axis):
        if axis == "x":
            return lambda way, step: {"det": det_index(signed(x, step, way, width), z, core, depth)}
        return lambda way, step: {"det": det_index(x, signed(z, step, way, depth), core, depth)}

    sizes, places = {"x": width, "z": depth}, {"x": x, "z": z}
    barrier = pltpu.get_barrier_semaphore()
    friends = [other]
    for axis, size in (("x", width), ("z", depth)):
        friends += [device(axis)(way, step) for step in range(1, size // 4 + 1) for way in (0, 1)]
    for friend in friends:
        pl.semaphore_signal(barrier, inc=1, device_id=friend, device_id_type=pl.DeviceIdType.MESH)
    pl.semaphore_wait(barrier, len(friends))
    links = Links(send_ref, recv_ref)

    def with_core(index, which):
        return index[:2] + (which,) + index[2:]

    def indices(first, start):
        second = "x" if first == "z" else "z"

        def order(dest, across):
            return (across, dest) if first == "z" else (dest, across)

        def wide(dest, l, lo, length):
            across = pl.ds(0, sizes[second]) if l is None else l
            return order(dest, across) + (pl.ds(start + lo, length), slice(None))

        def narrow(dest, l, lo, length):
            across = pl.ds(places[first], 1) if l is None else places[first]
            return order(across, dest) + (pl.ds(start + lo, length), slice(None))

        return second, wide, narrow

    def stream(name, first, start, rows, refs):
        second, wide, narrow = indices(first, start)
        left = [c for step in chunk_order(sizes[first]) for c in step]

        def base(dest):
            links.arrive((name, "core") + left.pop(0))

        base.ref = dense_ref
        base.index = lambda *key: with_core(wide(*key), core)

        def store(l, lo, index, total):
            begin, end = start + lo, start + lo + total.shape[0]
            while begin < end:
                box = begin // band
                stop = min(end, (box + 1) * band)
                part = total[begin - start - lo : stop - start - lo] / total_ref[pl.ds(box, 1), :]
                part = part.astype(jnp.bfloat16)
                all_ref[x, z, core, pl.ds(begin, stop - begin), :] = part
                coadd_ref[pl.ds(begin - box * band, stop - begin), pl.ds(box * TILE, TILE)] = part
                begin = stop

        def view(maker):
            return lambda origin, lo, length: all_ref.at[with_core(maker(origin, None, lo, length), core)]

        def nothing(origin, key):
            return None

        def across(origin, key):
            place = view(wide)(origin, 0, rows)
            links.start((name, "back", key), place, place, other)

        yield from ring_reduce(
            links, (name, 1), sizes[first], places[first], sizes[second], rows, wide, held_ref,
            refs[0], refs[1], device(first), base, None,
        )
        yield from ring_reduce(
            links, (name, 2), sizes[second], places[second], 1, rows, narrow, held_ref,
            refs[2], refs[3], device(second), None, store,
        )
        yield from ring_gather(
            links, (name, 3), sizes[second], places[second], rows, view(narrow), device(second), nothing
        )
        yield from ring_gather(
            links, (name, 4), sizes[first], places[first], rows, view(wide), device(first), across
        )

    firsts = {name: (first, start, rows) for name, first, start, rows in STREAMS}
    waiting = {name: chunk_order(sizes[firsts[name][0]]) for name in firsts}
    for name in ORDER:
        if not waiting[name]:
            continue
        first, start, rows = firsts[name]
        wide = indices(first, start)[1]
        for step, way in waiting[name].pop(0):
            index = wide(signed(places[first], step, way, sizes[first]), None, 0, rows)
            links.start((name, "core", step, way), dense_ref.at[with_core(index, 1 - core)], held_ref.at[index], other)

    runs = {}
    for number, (name, first, start, rows) in enumerate(STREAMS):
        runs[name] = stream(name, first, start, rows, buffers[4 * number : 4 * number + 4])
    for name in ORDER:
        next(runs[name], None)
    for run in runs.values():
        for _ in run:
            pass
    for key in list(links.copies):
        if key[1] == "back":
            links.arrive(key)
    links.finish()


def exchange(totals, dense, band, width, depth):
    rows = dense.shape[3]
    sizes = {"x": width, "z": depth}
    copies = 0
    scratch = []
    for name, first, start, length in STREAMS:
        size, other = sizes[first], width + depth - sizes[first]
        copies += 4 * (size + other) + 2 * size
        for places, lead in ((size, other), (other, 1)):
            scratch.append(pltpu.VMEM((places // 2 - 1, 2, lead, length, TILE), jnp.bfloat16))
            scratch.append(pltpu.VMEM((2, lead, length // 2, TILE), jnp.bfloat16))
    return pl.pallas_call(
        functools.partial(exchange_kernel, width, depth),
        in_specs=[pl.BlockSpec(memory_space=pltpu.VMEM)] * 2,
        out_specs=[pl.BlockSpec(memory_space=pltpu.VMEM)] * 2,
        out_shape=[
            jax.ShapeDtypeStruct(dense.shape, jnp.bfloat16),
            jax.ShapeDtypeStruct((band, rows // band * TILE), jnp.bfloat16),
        ],
        scratch_shapes=[
            pltpu.VMEM((width, depth, rows, TILE), jnp.bfloat16),
            pltpu.SemaphoreType.DMA((copies,)),
            pltpu.SemaphoreType.DMA((copies,)),
        ]
        + scratch,
        compiler_params=pltpu.CompilerParams(
            collective_id=0, has_side_effects=True, vmem_limit_bytes=40 << 20
        ),
        name="exchange",
    )(totals, dense)


def gather_match_kernel(
    reach,
    offsets,
    coef_ref,
    taps_ref,
    patch_ref,
    block_ref,
    index_ref,
    levels_ref,
    home_ref,
    images_hbm,
    rows_hbm,
    cols_hbm,
    out_hbm,
    total_ref,
    out_ref,
    images_ref,
    rows_ref,
    cols_ref,
    full_ref,
    halo_ref,
    window_ref,
    left_ref,
    table_ref,
    load_ref,
    save_ref,
    send_ref,
    recv_ref,
):
    count, band, side = images_hbm.shape
    half = band // 2
    size = full_ref.shape[1]
    me = lax.axis_index("row")
    beside = [signed(me, 1, way, size) for way in (0, 1)]

    def local(kind, image):
        source, target = ((images_hbm, images_ref), (cols_hbm, cols_ref), (rows_hbm, rows_ref))[kind]
        return pltpu.make_async_copy(source.at[image], target.at[image], load_ref.at[kind, image])

    def remote(kind, image, source, target, way):
        return pltpu.make_async_remote_copy(
            src_ref=source,
            dst_ref=target,
            send_sem=send_ref.at[kind, image],
            recv_sem=recv_ref.at[kind, image],
            device_id={"row": beside[way]},
            device_id_type=pl.DeviceIdType.MESH,
        )

    def own(image, way):
        place = full_ref.at[image, me]
        return remote(way, image, place, place, way)

    def forward(image, way):
        place = full_ref.at[image, beside[1 - way], pl.ds(way * half, half), :]
        return remote(2 + way, image, place, place, way)

    def edge(image, way):
        start = band - HALO if way == 0 else 0
        return remote(4 + way, image, rows_hbm.at[image, pl.ds(start, HALO), :], halo_ref.at[image, way], way)

    def save(image):
        slot = lax.rem(image, 2)
        return pltpu.make_async_copy(out_ref.at[slot], out_hbm.at[image], save_ref.at[slot])

    for kind in range(3):
        @pl.loop(0, count)
        def _(image):
            local(kind, image).start()

    barrier = pltpu.get_barrier_semaphore()
    for friend in beside:
        pl.semaphore_signal(barrier, inc=1, device_id={"row": friend}, device_id_type=pl.DeviceIdType.MESH)
    table_ref[...] = jnp.zeros_like(table_ref)
    keep = table_mask(2 * reach + 1)
    parts = tap_parts(taps_ref[...], offsets)
    visits = coef_ref.shape[1]
    first = jnp.where(me == 0, 0.0, 1.0)
    last = jnp.where(me == size - 1, 0.0, 1.0)
    pl.semaphore_wait(barrier, 2)

    @pl.loop(0, count + LAG)
    def _(step):
        @pl.when(step < count)
        def _():
            local(0, step).wait()
            local(1, step).wait()
            mapped = jnp.dot(images_ref[step], cols_ref[step], preferred_element_type=jnp.float32)
            full_ref[step, me] = mapped.astype(jnp.bfloat16)
            for way in (0, 1):
                own(step, way).start()
                edge(step, way).start()

        @pl.when(step == PASS_ON - 1)
        def _():
            denominators(patch_ref, block_ref, index_ref, levels_ref, home_ref, total_ref, out_ref.shape[1])

        @pl.when((step >= PASS_ON) & (step < count + PASS_ON))
        def _():
            image = step - PASS_ON
            for way in (0, 1):
                own(image, way).wait_recv()
                forward(image, way).start()

        @pl.when(step >= LAG)
        def _():
            image = step - LAG
            coef = coef_ref[image // visits, pl.ds(lax.rem(image, visits), 1), :]
            build_table(base_rows(coef, parts), keep, table_ref, offsets)
            local(2, image).wait()
            for way in (0, 1):
                forward(image, way).wait_recv()
                edge(image, way).wait_recv()
            rows = jnp.concatenate([halo_ref[image, 0], rows_ref[image], halo_ref[image, 1]], axis=0)
            full = full_ref[image].reshape(side, side)
            warped = jnp.dot(rows, full, preferred_element_type=jnp.float32)
            warped = jnp.concatenate(
                [warped[:HALO] * first, warped[HALO : HALO + band], warped[HALO + band :] * last], axis=0
            )
            @pl.when(image >= 2)
            def _():
                save(image - 2).wait()

            convolve(warped, reach, window_ref, left_ref, table_ref, out_ref, lax.rem(image, 2), offsets)
            save(image).start()

    for image in (count - 2, count - 1):
        save(image).wait()

    @pl.loop(0, count)
    def _(image):
        for way in (0, 1):
            own(image, way).wait_send()
            forward(image, way).wait_send()
            edge(image, way).wait_send()


def gather_match(coef, taps, patch, block, index, levels, home, images, rows, cols, size):
    count, band, side = images.shape
    reach = (taps.shape[1] - 1) // 2
    offsets = 2 * reach + GROUP
    tiles = side // TILE
    hbm = pl.BlockSpec(memory_space=pltpu.MemorySpace.HBM)
    vmem = pl.BlockSpec(memory_space=pltpu.VMEM)
    smem = pl.BlockSpec(memory_space=pltpu.SMEM)
    return pl.pallas_call(
        functools.partial(gather_match_kernel, reach, offsets),
        in_specs=[vmem, vmem, vmem, vmem, vmem, smem, vmem, hbm, hbm, hbm],
        out_specs=[hbm, vmem],
        out_shape=[
            jax.ShapeDtypeStruct((count, tiles, band, TILE), jnp.float32),
            jax.ShapeDtypeStruct((8, TILE), jnp.float32),
        ],
        scratch_shapes=[
            pltpu.VMEM((2, tiles, band, TILE), jnp.float32),
            pltpu.VMEM((count, band, side), jnp.bfloat16),
            pltpu.VMEM((count, band, side), jnp.bfloat16),
            pltpu.VMEM((count, side, side), jnp.bfloat16),
            pltpu.VMEM((count, size, band, side), jnp.bfloat16),
            pltpu.VMEM((count, 2, HALO, side), jnp.bfloat16),
            pltpu.VMEM((2 * tiles, band + 2 * HALO, TILE), jnp.float32),
            pltpu.VMEM((2 * tiles * (band // GROUP), offsets * TILE), jnp.bfloat16),
            pltpu.VMEM((offsets * TILE, 2 * TILE), jnp.bfloat16),
            pltpu.SemaphoreType.DMA((3, count)),
            pltpu.SemaphoreType.DMA((2,)),
            pltpu.SemaphoreType.DMA((6, count)),
            pltpu.SemaphoreType.DMA((6, count)),
        ],
        compiler_params=pltpu.CompilerParams(
            collective_id=1, has_side_effects=True, vmem_limit_bytes=58 << 20
        ),
        name="gather_match",
    )(coef, taps, patch, block, index, levels, home, images, rows, cols)


def per_device(
    images,
    warp_rows,
    warp_cols,
    psf_coef,
    taps,
    dest_patch,
    dest_block,
    weight_index,
    weight_table,
    patch_home,
):
    dets, visits, band, cols = images.shape
    tiles = cols // TILE
    count = dets * visits
    patches = patch_home.shape[0]
    row_size = lax.axis_size("row")
    patch = dest_patch.T
    block = dest_block.reshape(-1, TILE)
    index = weight_index.T

    matched, totals = gather_match(
        psf_coef,
        taps,
        patch,
        block,
        index,
        weight_table,
        patch_home[None],
        images.reshape(count, band, cols),
        warp_rows.reshape(count, band, cols),
        warp_cols.reshape(count, cols, cols),
        row_size,
    )
    dense, targets = collect(patch, block, index, weight_table, patch_home, matched, patches * tiles)
    depth = DEPTH
    width = patches // (2 * depth)
    shape = (width, depth, 2, tiles * band, TILE)
    templates, coadd = exchange(totals, dense.reshape(shape), band, width, depth)
    difference, coadd = subtract(targets, matched, templates.reshape(patches * tiles, band, TILE), coadd)
    return (difference.reshape(dets, visits, band, cols), coadd[None])


def solution(mesh):
    placed = (
        P("det", None, "row", None),
        P("det", None, "row", None),
        P("det", None, None, None),
        P("det", None, None),
        P(),
        P(),
        P(),
        P(),
        P(),
        P(),
    )
    return jax.shard_map(
        per_device,
        mesh=mesh,
        in_specs=placed,
        out_specs=(P("det", None, "row", None), P("det", "row", None)),
        check_vma=False,
    )
```

```python
import functools

import jax
import jax.numpy as jnp
from jax import lax
from jax.experimental import pallas as pl
from jax.experimental.pallas import tpu as pltpu
from jax.sharding import PartitionSpec as P

TILE = 128
HALF = 64
HALO = 16
GROUP = 4
DEPTH = 8
STREAMS = (("a", "z", 0, 32), ("c", "z", 32, 64), ("b", "x", 96, 64), ("d", "x", 160, 64), ("e", "x", 224, 64))
ORDER = "bcedbadecbadbecadcbeadcbeacdabecdaecdbaecbdea"
PASS_ON = 2
LAG = 4
SUBTRACT_STEPS = 3


def one_hot(mask):
    return jnp.where(mask, 1.0, 0.0).astype(jnp.bfloat16)


def iota2(rows, cols, axis):
    return lax.broadcasted_iota(jnp.int32, (rows, cols), axis)


def tap_parts(taps, offsets):
    kernels, span = taps.shape
    shift = iota2(offsets, span, 0) - iota2(offsets, span, 1)

    def by_offset(late):
        pick = jnp.where(shift == late, 1.0, 0.0)
        return lax.dot_general(
            pick, taps, (((1,), (1,)), ((), ())), precision=lax.Precision.HIGHEST, preferred_element_type=jnp.float32
        )

    tap, lane = iota2(span, TILE, 0), iota2(span, TILE, 1)
    half = taps.astype(jnp.bfloat16)

    def placed(mask):
        return jnp.dot(half, one_hot(mask), preferred_element_type=jnp.float32).astype(jnp.bfloat16)

    here = placed((lane + tap == TILE) | ((tap == 0) & (lane == 0)))
    there = placed(lane + tap == HALF)
    return by_offset(0), by_offset(1), here, there


def base_rows(coef, parts):
    lead, late, here, there = parts
    left = jnp.dot((coef * lead).astype(jnp.bfloat16), here, preferred_element_type=jnp.float32)
    return left + jnp.dot((coef * late).astype(jnp.bfloat16), there, preferred_element_type=jnp.float32)


def denominators(patch_ref, block_ref, index_ref, table_ref, home_ref, out_ref, boxes):
    me = lax.axis_index("det")
    homes = home_ref[...]
    mine = jnp.sum(jnp.where(homes == me, iota2(1, homes.shape[1], 1), 0), axis=1, keepdims=True)
    visits, dets = index_ref.shape
    groups = dets // TILE
    period = visits * boxes
    row, lane = iota2(TILE, TILE, 0), iota2(TILE, TILE, 1)
    blank = jnp.zeros((8 - groups, TILE), jnp.float32)
    levels = []
    for visit in range(visits):
        parts = [index_ref[pl.ds(visit, 1), pl.ds(g * TILE, TILE)].astype(jnp.float32) for g in range(groups)]
        levels.append(jnp.concatenate(parts + [blank], axis=0).astype(jnp.bfloat16))
    sums = [jnp.zeros((groups, TILE), jnp.float32) for _ in range(boxes)]
    for k in range(period):
        level = jnp.zeros((8, TILE), jnp.float32)
        for visit in range(visits):
            gap = lane - period * row + (TILE * k - boxes * visit)
            level = level + jnp.dot(
                levels[visit], one_hot((gap >= 0) & (gap < boxes)), preferred_element_type=jnp.float32
            )
        level = level[:groups]
        weight = jnp.zeros((groups, TILE), jnp.float32)
        for n in range(table_ref.shape[0]):
            weight = jnp.where(level == float(n), table_ref[n], weight)
        patch = jnp.concatenate(
            [patch_ref[:, pl.ds((g * period + k) * TILE, TILE)] for g in range(groups)], axis=0
        )
        block = jnp.concatenate([block_ref[pl.ds(g * period + k, 1), :] for g in range(groups)], axis=0)
        for box in range(boxes):
            sums[box] = sums[box] + jnp.where((patch == mine) & (block == box), weight, 0.0)
    for box in range(boxes):
        total = jnp.sum(jnp.sum(sums[box], axis=0, keepdims=True), axis=1, keepdims=True)
        out_ref[pl.ds(box, 1), :] = jnp.broadcast_to(jnp.maximum(total, 1.0), (1, TILE))


def build_table(base, keep, table_ref, offsets):
    for t in range(offsets - 2):
        row = jnp.broadcast_to(base[t : t + 1], keep.shape)
        band = pltpu.roll(row, 0, 1, stride=1, stride_axis=0)
        band = jnp.where(keep, band, 0.0).astype(jnp.bfloat16)
        table_ref[pl.ds(t * TILE, keep.shape[0]), pl.ds(0, TILE)] = band
        table_ref[pl.ds((t + 2) * TILE, keep.shape[0]), pl.ds(TILE, TILE)] = band


def table_mask(span):
    rows = lax.broadcasted_iota(jnp.int32, (96, TILE), 0)
    lanes = lax.broadcasted_iota(jnp.int32, (96, TILE), 1)
    gap = rows - jnp.where(lanes >= HALF, lanes - HALF, lanes)
    return (gap >= 0) & (gap < span)


def convolve(warped, reach, window_ref, left_ref, table_ref, out_ref, image, offsets):
    rows, cols = warped.shape
    wide = jnp.concatenate([warped, jnp.zeros((rows, TILE), jnp.float32)], axis=1)
    even = pltpu.roll(wide, reach, 1)
    odd = pltpu.roll(wide, cols + TILE + reach - HALF, 1)
    tiles = cols // TILE
    groups = out_ref.shape[2] // GROUP
    for tile in range(tiles):
        window_ref[2 * tile] = even[:, tile * TILE : (tile + 1) * TILE]
        window_ref[2 * tile + 1] = odd[:, tile * TILE : (tile + 1) * TILE]
    for offset in range(offsets):
        start = HALO - reach + offset
        parts = [window_ref[w, pl.ds(start, groups, stride=GROUP), :] for w in range(2 * tiles)]
        left_ref[:, pl.ds(offset * TILE, TILE)] = jnp.concatenate(parts, axis=0).astype(jnp.bfloat16)
    product = jnp.dot(left_ref[...], table_ref[...], preferred_element_type=jnp.float32)
    low = lax.broadcasted_iota(jnp.int32, (groups, TILE), 1) < HALF
    for tile in range(tiles):
        for pair in range(2):
            first = product[(2 * tile) * groups : (2 * tile + 1) * groups, pair * TILE : (pair + 1) * TILE]
            second = product[(2 * tile + 1) * groups : (2 * tile + 2) * groups, pair * TILE : (pair + 1) * TILE]
            upper = jnp.where(low, first, pltpu.roll(second, HALF, 1))
            lower = jnp.where(low, pltpu.roll(first, HALF, 1), second)
            out_ref[image, tile, pl.ds(2 * pair, groups, stride=GROUP), :] = upper
            out_ref[image, tile, pl.ds(2 * pair + 1, groups, stride=GROUP), :] = lower


def collect_kernel(count, patch_ref, block_ref, index_ref, levels_ref, home_ref, matched_ref, dense_ref, target_ref):
    dets, tiles = count
    visits = index_ref.shape[0]
    me = lax.axis_index("det")
    dense_ref[...] = jnp.zeros_like(dense_ref)

    @pl.loop(0, dets)
    def _(det):
        for visit in range(visits):
            weight = levels_ref[index_ref[visit, me * dets + det]]
            for tile in range(tiles):
                local = (det * visits + visit) * tiles + tile
                piece = me * dets * visits * tiles + local
                row, lane = piece // TILE, lax.rem(piece, TILE)
                target = home_ref[patch_ref[0, piece]] * tiles + block_ref[row, lane]
                target_ref[local] = target
                value = matched_ref[det * visits + visit, tile].astype(jnp.float32)
                value = (weight * value).astype(jnp.bfloat16)
                held = dense_ref[target].astype(jnp.float32)
                dense_ref[target] = (held + value.astype(jnp.float32)).astype(jnp.bfloat16)


def collect(patch, block, index, levels, home, matched, boxes):
    images, tiles, band, _ = matched.shape
    smem = pl.BlockSpec(memory_space=pltpu.SMEM)
    vmem = pl.BlockSpec(memory_space=pltpu.VMEM)
    return pl.pallas_call(
        functools.partial(collect_kernel, (images // index.shape[0], tiles)),
        in_specs=[smem] * 5 + [vmem],
        out_specs=[vmem, smem],
        out_shape=[
            jax.ShapeDtypeStruct((boxes, band, TILE), jnp.bfloat16),
            jax.ShapeDtypeStruct((images * tiles,), jnp.int32),
        ],
        compiler_params=pltpu.CompilerParams(vmem_limit_bytes=32 << 20),
        name="collect",
    )(patch, block, index, levels, home, matched)


def subtract_kernel(tiles, target_ref, matched_ref, template_ref, coadd_ref, out_ref, coadd_out):
    step = pl.program_id(0)
    images = out_ref.shape[0]

    @pl.when(step == 0)
    def _():
        coadd_out[...] = coadd_ref[...]

    @pl.loop(0, images)
    def _(local):
        image = step * images + local
        for tile in range(tiles):
            template = template_ref[target_ref[image * tiles + tile]].astype(jnp.float32)
            value = matched_ref[image, tile].astype(jnp.float32) - template
            out_ref[local, :, pl.ds(tile * TILE, TILE)] = value.astype(jnp.bfloat16)


def subtract(targets, matched, templates, coadd):
    images, tiles, band, _ = matched.shape
    steps = SUBTRACT_STEPS
    vmem = pl.BlockSpec(memory_space=pltpu.VMEM)
    return pl.pallas_call(
        functools.partial(subtract_kernel, tiles),
        grid=(steps,),
        in_specs=[pl.BlockSpec(memory_space=pltpu.SMEM), vmem, vmem, vmem],
        out_specs=[
            pl.BlockSpec((images // steps, band, tiles * TILE), lambda i: (i, 0, 0)),
            pl.BlockSpec(coadd.shape, lambda i: (0, 0)),
        ],
        out_shape=[
            jax.ShapeDtypeStruct((images, band, tiles * TILE), jnp.bfloat16),
            jax.ShapeDtypeStruct(coadd.shape, jnp.bfloat16),
        ],
        compiler_params=pltpu.CompilerParams(vmem_limit_bytes=32 << 20),
        name="subtract",
    )(targets, matched, templates, coadd)


def det_index(x, z, core, depth):
    return (x * depth + z) * 2 + core


class Links:
    def __init__(self, send_ref, recv_ref):
        self.send_ref, self.recv_ref = send_ref, recv_ref
        self.copies = {}

    def start(self, key, source, target, device):
        index = len(self.copies)
        copy = pltpu.make_async_remote_copy(
            src_ref=source,
            dst_ref=target,
            send_sem=self.send_ref.at[index],
            recv_sem=self.recv_ref.at[index],
            device_id=device,
            device_id_type=pl.DeviceIdType.MESH,
        )
        copy.start()
        self.copies[key] = copy

    def arrive(self, key):
        self.copies[key].wait_recv()

    def finish(self):
        for copy in self.copies.values():
            copy.wait_send()


def signed(place, step, way, size):
    return lax.rem(place + size + (step if way == 0 else -step), size)


def adder(dest_at, lead, half, held_ref, base):
    def add(dest, extras, store):
        if base is not None:
            base(dest)

        def body(l, carry):
            for lo in (0, half):
                index = dest_at(dest, l, lo, half)
                total = held_ref[index].astype(jnp.float32)
                if base is not None:
                    total = total + base.ref[base.index(dest, l, lo, half)].astype(jnp.float32)
                for ref, way, from_half in extras:
                    if not from_half:
                        total = total + ref[way, l, pl.ds(lo, half), :].astype(jnp.float32)
                    elif lo == way * half:
                        total = total + ref[way, l].astype(jnp.float32)
                store(l, lo, index, total)
            return carry

        lax.fori_loop(0, lead, body, 0)

    return add


def ring_reduce(links, tag, size, place, lead, rows, at, held_ref, whole_ref, half_ref, device, base, finish):
    middle, half = size // 2, rows // 2
    add = adder(at, lead, half, held_ref, base)

    def put(l, lo, index, total):
        held_ref[index] = total.astype(jnp.bfloat16)

    def send(key, dest, buffer, way, distance, lo=0, length=rows):
        links.start((tag, way, key), held_ref.at[at(dest, None, lo, length)], buffer, device(way, distance))

    relay = middle // 2
    far = signed(place, middle, 0, size)
    if base is not None:
        add(far, [], put)
    for way in (0, 1):
        send(middle, far, half_ref.at[way], way, relay, way * half, half)
    for step in range(middle - 1, 0, -1):
        if step == relay:
            continue
        for way in (0, 1):
            dest = signed(place, step, way, size)
            if base is not None:
                add(dest, [], put)
            send(step, dest, whole_ref.at[step - 1, way], way, step - relay if step > relay else step)
    yield
    for way in (0, 1):
        dest = signed(place, relay, way, size)
        sources = [(half_ref, way, True)]
        links.arrive((tag, way, middle))
        for step in range(relay + 1, middle):
            links.arrive((tag, way, step))
            sources.append((whole_ref.at[step - 1], way, False))
        add(dest, sources, put)
        send(relay, dest, whole_ref.at[relay - 1, way], way, relay)
    yield
    last = [(step, way) for step in range(1, relay + 1) for way in (0, 1)]
    for step, way in last:
        links.arrive((tag, way, step))
    add(place, [(whole_ref.at[step - 1], way, False) for step, way in last], put if finish is None else finish)


def ring_gather(links, tag, size, place, rows, view, device, arrived):
    middle, half = size // 2, rows // 2
    relay = middle // 2

    def send(key, origin, way, distance, lo=0, length=rows):
        part = view(origin, lo, length)
        links.start((tag, way, key), part, part, device(way, distance))

    for step in range(relay, 0, -1):
        for way in (0, 1):
            send(step, place, way, step)
    arrived(place, 0)
    yield
    for way in (0, 1):
        origin = signed(place, relay, 1 - way, size)
        links.arrive((tag, way, relay))
        for step in range(relay + 1, middle):
            send(step, origin, way, step - relay)
        send(middle, origin, way, relay, way * half, half)
        arrived(origin, (relay, way))
    for step in range(1, middle):
        if step < relay:
            for way in (0, 1):
                links.arrive((tag, way, step))
                arrived(signed(place, step, 1 - way, size), (step, way))
    yield
    for step in range(relay + 1, middle):
        for way in (0, 1):
            links.arrive((tag, way, step))
            arrived(signed(place, step, 1 - way, size), (step, way))
    for way in (0, 1):
        links.arrive((tag, way, middle))
    arrived(signed(place, middle, 0, size), middle)


def chunk_order(size):
    middle = size // 2
    relay = middle // 2
    first = [(middle, 0)] + [(step, way) for step in range(middle - 1, 0, -1) if step != relay for way in (0, 1)]
    return [first, [(relay, 0), (relay, 1)], [(0, 0)]]


def exchange_kernel(width, depth, total_ref, dense_ref, all_ref, coadd_ref, held_ref, send_ref, recv_ref, *buffers):
    band = coadd_ref.shape[0]
    me = lax.axis_index("det")
    core = lax.rem(me, 2)
    z = lax.rem(me // 2, depth)
    x = me // (2 * depth)
    other = {"det": det_index(x, z, 1 - core, depth)}

    def device(axis):
        if axis == "x":
            return lambda way, step: {"det": det_index(signed(x, step, way, width), z, core, depth)}
        return lambda way, step: {"det": det_index(x, signed(z, step, way, depth), core, depth)}

    sizes, places = {"x": width, "z": depth}, {"x": x, "z": z}
    barrier = pltpu.get_barrier_semaphore()
    friends = [other]
    for axis, size in (("x", width), ("z", depth)):
        friends += [device(axis)(way, step) for step in range(1, size // 4 + 1) for way in (0, 1)]
    for friend in friends:
        pl.semaphore_signal(barrier, inc=1, device_id=friend, device_id_type=pl.DeviceIdType.MESH)
    pl.semaphore_wait(barrier, len(friends))
    links = Links(send_ref, recv_ref)

    def with_core(index, which):
        return index[:2] + (which,) + index[2:]

    def indices(first, start):
        second = "x" if first == "z" else "z"

        def order(dest, across):
            return (across, dest) if first == "z" else (dest, across)

        def wide(dest, l, lo, length):
            across = pl.ds(0, sizes[second]) if l is None else l
            return order(dest, across) + (pl.ds(start + lo, length), slice(None))

        def narrow(dest, l, lo, length):
            across = pl.ds(places[first], 1) if l is None else places[first]
            return order(across, dest) + (pl.ds(start + lo, length), slice(None))

        return second, wide, narrow

    def stream(name, first, start, rows, refs):
        second, wide, narrow = indices(first, start)
        left = [c for step in chunk_order(sizes[first]) for c in step]

        def base(dest):
            links.arrive((name, "core") + left.pop(0))

        base.ref = dense_ref
        base.index = lambda *key: with_core(wide(*key), core)

        def store(l, lo, index, total):
            begin, end = start + lo, start + lo + total.shape[0]
            while begin < end:
                box = begin // band
                stop = min(end, (box + 1) * band)
                part = total[begin - start - lo : stop - start - lo] / total_ref[pl.ds(box, 1), :]
                part = part.astype(jnp.bfloat16)
                all_ref[x, z, core, pl.ds(begin, stop - begin), :] = part
                coadd_ref[pl.ds(begin - box * band, stop - begin), pl.ds(box * TILE, TILE)] = part
                begin = stop

        def view(maker):
            return lambda origin, lo, length: all_ref.at[with_core(maker(origin, None, lo, length), core)]

        def nothing(origin, key):
            return None

        def across(origin, key):
            place = view(wide)(origin, 0, rows)
            links.start((name, "back", key), place, place, other)

        yield from ring_reduce(
            links, (name, 1), sizes[first], places[first], sizes[second], rows, wide, held_ref,
            refs[0], refs[1], device(first), base, None,
        )
        yield from ring_reduce(
            links, (name, 2), sizes[second], places[second], 1, rows, narrow, held_ref,
            refs[2], refs[3], device(second), None, store,
        )
        yield from ring_gather(
            links, (name, 3), sizes[second], places[second], rows, view(narrow), device(second), nothing
        )
        yield from ring_gather(
            links, (name, 4), sizes[first], places[first], rows, view(wide), device(first), across
        )

    firsts = {name: (first, start, rows) for name, first, start, rows in STREAMS}
    waiting = {name: chunk_order(sizes[firsts[name][0]]) for name in firsts}
    for name in ORDER:
        if not waiting[name]:
            continue
        first, start, rows = firsts[name]
        wide = indices(first, start)[1]
        for step, way in waiting[name].pop(0):
            index = wide(signed(places[first], step, way, sizes[first]), None, 0, rows)
            links.start((name, "core", step, way), dense_ref.at[with_core(index, 1 - core)], held_ref.at[index], other)

    runs = {}
    for number, (name, first, start, rows) in enumerate(STREAMS):
        runs[name] = stream(name, first, start, rows, buffers[4 * number : 4 * number + 4])
    for name in ORDER:
        next(runs[name], None)
    for run in runs.values():
        for _ in run:
            pass
    for key in list(links.copies):
        if key[1] == "back":
            links.arrive(key)
    links.finish()


def exchange(totals, dense, band, width, depth):
    rows = dense.shape[3]
    sizes = {"x": width, "z": depth}
    copies = 0
    scratch = []
    for name, first, start, length in STREAMS:
        size, other = sizes[first], width + depth - sizes[first]
        copies += 4 * (size + other) + 2 * size
        for places, lead in ((size, other), (other, 1)):
            scratch.append(pltpu.VMEM((places // 2 - 1, 2, lead, length, TILE), jnp.bfloat16))
            scratch.append(pltpu.VMEM((2, lead, length // 2, TILE), jnp.bfloat16))
    return pl.pallas_call(
        functools.partial(exchange_kernel, width, depth),
        in_specs=[pl.BlockSpec(memory_space=pltpu.VMEM)] * 2,
        out_specs=[pl.BlockSpec(memory_space=pltpu.VMEM)] * 2,
        out_shape=[
            jax.ShapeDtypeStruct(dense.shape, jnp.bfloat16),
            jax.ShapeDtypeStruct((band, rows // band * TILE), jnp.bfloat16),
        ],
        scratch_shapes=[
            pltpu.VMEM((width, depth, rows, TILE), jnp.bfloat16),
            pltpu.SemaphoreType.DMA((copies,)),
            pltpu.SemaphoreType.DMA((copies,)),
        ]
        + scratch,
        compiler_params=pltpu.CompilerParams(
            collective_id=0, has_side_effects=True, vmem_limit_bytes=40 << 20
        ),
        name="exchange",
    )(totals, dense)


def gather_match_kernel(
    reach,
    offsets,
    coef_ref,
    taps_ref,
    patch_ref,
    block_ref,
    index_ref,
    levels_ref,
    home_ref,
    images_hbm,
    rows_hbm,
    cols_hbm,
    out_hbm,
    total_ref,
    out_ref,
    saved_ref,
    images_ref,
    rows_ref,
    cols_ref,
    full_ref,
    halo_ref,
    window_ref,
    left_ref,
    table_ref,
    load_ref,
    save_ref,
    send_ref,
    recv_ref,
):
    count, band, side = images_hbm.shape
    half = band // 2
    size = full_ref.shape[1]
    me = lax.axis_index("row")
    beside = [signed(me, 1, way, size) for way in (0, 1)]

    def local(kind, image):
        source, target = ((images_hbm, images_ref), (cols_hbm, cols_ref), (rows_hbm, rows_ref))[kind]
        return pltpu.make_async_copy(source.at[image], target.at[image], load_ref.at[kind, image])

    def remote(kind, image, source, target, way):
        return pltpu.make_async_remote_copy(
            src_ref=source,
            dst_ref=target,
            send_sem=send_ref.at[kind, image],
            recv_sem=recv_ref.at[kind, image],
            device_id={"row": beside[way]},
            device_id_type=pl.DeviceIdType.MESH,
        )

    def own(image, way):
        place = full_ref.at[image, me]
        return remote(way, image, place, place, way)

    def forward(image, way):
        place = full_ref.at[image, beside[1 - way], pl.ds(way * half, half), :]
        return remote(2 + way, image, place, place, way)

    def edge(image, way):
        start = band - HALO if way == 0 else 0
        return remote(4 + way, image, rows_hbm.at[image, pl.ds(start, HALO), :], halo_ref.at[image, way], way)

    def save(image):
        slot = lax.rem(image, 2)
        return pltpu.make_async_copy(saved_ref.at[slot], out_hbm.at[image], save_ref.at[slot])

    for kind in range(3):
        @pl.loop(0, count)
        def _(image):
            local(kind, image).start()

    barrier = pltpu.get_barrier_semaphore()
    for friend in beside:
        pl.semaphore_signal(barrier, inc=1, device_id={"row": friend}, device_id_type=pl.DeviceIdType.MESH)
    table_ref[...] = jnp.zeros_like(table_ref)
    keep = table_mask(2 * reach + 1)
    parts = tap_parts(taps_ref[...], offsets)
    visits = coef_ref.shape[1]
    first = jnp.where(me == 0, 0.0, 1.0)
    last = jnp.where(me == size - 1, 0.0, 1.0)
    pl.semaphore_wait(barrier, 2)

    @pl.loop(0, count + LAG)
    def _(step):
        @pl.when(step < count)
        def _():
            local(0, step).wait()
            local(1, step).wait()
            mapped = jnp.dot(images_ref[step], cols_ref[step], preferred_element_type=jnp.float32)
            full_ref[step, me] = mapped.astype(jnp.bfloat16)
            for way in (0, 1):
                own(step, way).start()
                edge(step, way).start()

        @pl.when(step == PASS_ON - 1)
        def _():
            denominators(patch_ref, block_ref, index_ref, levels_ref, home_ref, total_ref, out_ref.shape[1])

        @pl.when((step >= PASS_ON) & (step < count + PASS_ON))
        def _():
            image = step - PASS_ON
            for way in (0, 1):
                own(image, way).wait_recv()
                forward(image, way).start()

        @pl.when(step >= LAG)
        def _():
            image = step - LAG
            coef = coef_ref[image // visits, pl.ds(lax.rem(image, visits), 1), :]
            build_table(base_rows(coef, parts), keep, table_ref, offsets)
            local(2, image).wait()
            for way in (0, 1):
                forward(image, way).wait_recv()
                edge(image, way).wait_recv()
            rows = jnp.concatenate([halo_ref[image, 0], rows_ref[image], halo_ref[image, 1]], axis=0)
            full = full_ref[image].reshape(side, side)
            warped = jnp.dot(rows, full, preferred_element_type=jnp.float32)
            warped = jnp.concatenate(
                [warped[:HALO] * first, warped[HALO : HALO + band], warped[HALO + band :] * last], axis=0
            )
            @pl.when(image >= 2)
            def _():
                save(image - 2).wait()

            convolve(warped, reach, window_ref, left_ref, table_ref, out_ref, 0, offsets)
            saved_ref[lax.rem(image, 2)] = out_ref[0].astype(jnp.bfloat16)
            save(image).start()

    for image in (count - 2, count - 1):
        save(image).wait()

    @pl.loop(0, count)
    def _(image):
        for way in (0, 1):
            own(image, way).wait_send()
            forward(image, way).wait_send()
            edge(image, way).wait_send()


def gather_match(coef, taps, patch, block, index, levels, home, images, rows, cols, size):
    count, band, side = images.shape
    reach = (taps.shape[1] - 1) // 2
    offsets = 2 * reach + GROUP
    tiles = side // TILE
    hbm = pl.BlockSpec(memory_space=pltpu.MemorySpace.HBM)
    vmem = pl.BlockSpec(memory_space=pltpu.VMEM)
    smem = pl.BlockSpec(memory_space=pltpu.SMEM)
    return pl.pallas_call(
        functools.partial(gather_match_kernel, reach, offsets),
        in_specs=[vmem, vmem, vmem, vmem, vmem, smem, vmem, hbm, hbm, hbm],
        out_specs=[hbm, vmem],
        out_shape=[
            jax.ShapeDtypeStruct((count, tiles, band, TILE), jnp.bfloat16),
            jax.ShapeDtypeStruct((8, TILE), jnp.float32),
        ],
        scratch_shapes=[
            pltpu.VMEM((1, tiles, band, TILE), jnp.float32),
            pltpu.VMEM((2, tiles, band, TILE), jnp.bfloat16),
            pltpu.VMEM((count, band, side), jnp.bfloat16),
            pltpu.VMEM((count, band, side), jnp.bfloat16),
            pltpu.VMEM((count, side, side), jnp.bfloat16),
            pltpu.VMEM((count, size, band, side), jnp.bfloat16),
            pltpu.VMEM((count, 2, HALO, side), jnp.bfloat16),
            pltpu.VMEM((2 * tiles, band + 2 * HALO, TILE), jnp.float32),
            pltpu.VMEM((2 * tiles * (band // GROUP), offsets * TILE), jnp.bfloat16),
            pltpu.VMEM((offsets * TILE, 2 * TILE), jnp.bfloat16),
            pltpu.SemaphoreType.DMA((3, count)),
            pltpu.SemaphoreType.DMA((2,)),
            pltpu.SemaphoreType.DMA((6, count)),
            pltpu.SemaphoreType.DMA((6, count)),
        ],
        compiler_params=pltpu.CompilerParams(
            collective_id=1, has_side_effects=True, vmem_limit_bytes=58 << 20
        ),
        name="gather_match",
    )(coef, taps, patch, block, index, levels, home, images, rows, cols)


def per_device(
    images,
    warp_rows,
    warp_cols,
    psf_coef,
    taps,
    dest_patch,
    dest_block,
    weight_index,
    weight_table,
    patch_home,
):
    dets, visits, band, cols = images.shape
    tiles = cols // TILE
    count = dets * visits
    patches = patch_home.shape[0]
    row_size = lax.axis_size("row")
    patch = dest_patch.T
    block = dest_block.reshape(-1, TILE)
    index = weight_index.T

    matched, totals = gather_match(
        psf_coef,
        taps,
        patch,
        block,
        index,
        weight_table,
        patch_home[None],
        images.reshape(count, band, cols),
        warp_rows.reshape(count, band, cols),
        warp_cols.reshape(count, cols, cols),
        row_size,
    )
    dense, targets = collect(patch, block, index, weight_table, patch_home, matched, patches * tiles)
    depth = DEPTH
    width = patches // (2 * depth)
    shape = (width, depth, 2, tiles * band, TILE)
    templates, coadd = exchange(totals, dense.reshape(shape), band, width, depth)
    difference, coadd = subtract(targets, matched, templates.reshape(patches * tiles, band, TILE), coadd)
    return (difference.reshape(dets, visits, band, cols), coadd[None])


def solution(mesh):
    placed = (
        P("det", None, "row", None),
        P("det", None, "row", None),
        P("det", None, None, None),
        P("det", None, None),
        P(),
        P(),
        P(),
        P(),
        P(),
        P(),
    )
    return jax.shard_map(
        per_device,
        mesh=mesh,
        in_specs=placed,
        out_specs=(P("det", None, "row", None), P("det", "row", None)),
        check_vma=False,
    )
```
